256 devices in a mesh: seq: 16 (over x_hi, y, core), fsdp: 16 (over x_lo, z).
Axes of the slice: x: 4 (x_hi: 2, x_lo: 2; x = x_hi * 2 + x_lo), y: 4, z: 8, core: 2. Of those that a mesh axis runs over, the one named last changes fastest.
Arguments:
- query: bfloat16 [16, 2560, 4096], P('fsdp', 'seq'), may hold values from -6 to 6
- key: bfloat16 [16, 2560, 4096], P('fsdp', 'seq'), may hold values from -6 to 6
- value: bfloat16 [16, 2560, 4096], P('fsdp', 'seq'), may hold values from -6 to 6
- stream: bfloat16 [16, 2560, 4096], P('fsdp', 'seq'), may hold values from -6 to 6
- targets: int32 [16, 2560], P('fsdp', 'seq'), may hold values from 0 to 3
- short_filter: float32 [7, 3, 2048], replicated, may hold values from -2 to 2
- med_filter: bfloat16 [128, 128], replicated, may hold values from -0.5 to 0.5
- out_weight: bfloat16 [2048, 2048], P('fsdp'), may hold values from -0.125 to 0.125
- head: float32 [4, 2048], replicated, may hold values from -0.09375 to 0.09375
Outputs:
- query_grad: bfloat16 [16, 2560, 4096], P('fsdp', 'seq')
- key_grad: bfloat16 [16, 2560, 4096], P('fsdp', 'seq')
- value_grad: bfloat16 [16, 2560, 4096], P('fsdp', 'seq')
- out_grad: float32 [2048, 2048], P('fsdp')
The draws below stay inside these ranges and needn't reach their ends.
All inputs are finite; a program needn't handle non-finite values.
Results may differ from the reference program's by a relative error of at most 0.022.
Values may be sent and summed in bfloat16 or wider, within the bound.
No kernel may reach another device: no remote copies, remote signals or barrier semaphores. Data moves between devices by JAX's collectives and lax.ppermute only.
A program may use at most 192 MiB of HBM per device.

```python
import jax
import jax.numpy as jnp
from jax import lax

D = 4096
H = 2048
CPG = 16
GROUPS = 128
SHORT = 7
MED = 128
NUC = 4
GENOMES = 16
SEQ = 2560


def set_ends(array, key, low, top_value):
    longest = array.shape.index(max(array.shape))
    spots = []
    for shift in (0, 1):
        where = [jax.random.randint(jax.random.fold_in(key, axis), (), 0, length) for axis, length in enumerate(array.shape)]
        where[longest] = (where[longest] + shift) % array.shape[longest]
        spots.append(tuple(where))
    return array.at[spots[0]].set(low).at[spots[1]].set(top_value)


def spiked(drawn, key, source, target, blocks, factor):
    def block_of(axis_at):
        return (jnp.arange(drawn.shape[axis_at]) // (drawn.shape[axis_at] // blocks)).reshape((-1,) + (1,) * (drawn.ndim - 1 - axis_at))

    first = jax.random.permutation(key, blocks)[block_of(target)]
    other_side = (block_of(target) + blocks // 2) % blocks
    return jnp.where((block_of(source) == first) | (block_of(source) == other_side), factor * drawn, drawn)


def shard_levels(key, dims, pieces, least, top_value):
    def one(dim, shards_of):
        steps = jax.random.uniform(jax.random.fold_in(jax.random.fold_in(key, 6), dim), (shards_of,), jnp.float32, least / len(pieces), top_value / len(pieces))
        return jnp.repeat(jnp.exp(steps), dims[dim] // shards_of).reshape((-1,) + (1,) * (len(dims) - dim - 1))

    gain = one(*pieces[0])
    for cut in pieces[1:]:
        gain = gain * one(*cut)
    return gain


def normal_values(rng, extent, deviation, most, split=(), kind=jnp.bfloat16):
    loudness = shard_levels(rng, extent, split, -0.22, 0.18) if split else 1.0
    values = jax.random.normal(rng, extent, jnp.float32) * deviation * loudness
    return jnp.minimum(jnp.maximum(values, -most), most).astype(kind)


def gaussian_with(rng, shape, spread, bound, shards, heavy, kind=jnp.bfloat16):
    values = spread * jax.random.normal(rng, shape, jnp.float32)
    if shards:
        values = values * shard_levels(rng, shape, shards, -0.22, 0.18)
    return jnp.clip(spiked(values, jax.random.fold_in(rng, 3), *heavy), -bound, bound).astype(kind)


def setup_inputs(seed: int = 0) -> dict:
    streams_of = jax.random.split(jax.random.key(seed), 10)
    return {
        "query": gaussian_with(streams_of[0], (GENOMES, SEQ, D), 1.0, 6.0, ((0, 16), (1, 16)), (0, 2, 16, 2.0)),
        "key": normal_values(streams_of[1], (GENOMES, SEQ, D), 1.0, 6.0, ((0, 16), (1, 16))),
        "value": normal_values(streams_of[2], (GENOMES, SEQ, D), 1.0, 6.0, ((0, 16), (1, 16))),
        "stream": normal_values(streams_of[3], (GENOMES, SEQ, D), 1.0, 6.0, ((0, 16), (1, 16))),
        "targets": set_ends(jax.random.randint(streams_of[4], (GENOMES, SEQ), 0, NUC), jax.random.fold_in(streams_of[4], 1), 0, NUC - 1).astype(jnp.int32),
        "short_filter": normal_values(streams_of[5], (SHORT, 3, H), SHORT ** -0.5, 2.0, (), jnp.float32),
        "med_filter": normal_values(streams_of[6], (MED, GROUPS), MED ** -0.5, 0.5),
        "out_weight": normal_values(streams_of[7], (H, H), H ** -0.5, 0.125, ((0, 16),)),
        "head": normal_values(streams_of[8], (NUC, H), D ** -0.5, 0.09375, (), jnp.float32),
    }


loss_scale = 64.0


def causal_fft(signal, conv_taps):
    length = signal.shape[0]
    size_total = length + conv_taps.shape[0]
    spectrum = jnp.fft.rfft(signal, n=size_total, axis=0) * jnp.fft.rfft(conv_taps, n=size_total, axis=0)
    return jnp.fft.irfft(spectrum, n=size_total, axis=0)[:length]


def causal_short(signal, conv_taps):
    length = signal.shape[0]
    summed = conv_taps[0] * signal
    for offset in range(1, conv_taps.shape[0]):
        moved = jnp.pad(signal, ((offset, 0), (0, 0)))[:length]
        summed = summed + conv_taps[offset] * moved
    return summed


def orient(signal, flip_first, half_width):
    if flip_first:
        return jnp.concatenate([signal[::-1, :half_width], signal[:, half_width:]], axis=1)
    return jnp.concatenate([signal[:, :half_width], signal[::-1, half_width:]], axis=1)


def directed(signal, conv_taps, backward, use_fft):
    half_width = signal.shape[1] // 2
    both_taps = jnp.concatenate([conv_taps, conv_taps], axis=1)
    turned = orient(signal, backward, half_width)
    if use_fft:
        result = causal_fft(turned, both_taps)
    else:
        result = causal_short(turned, both_taps)
    return orient(result, backward, half_width)


def one_genome(query_g, key_g, value_g, stream_g, target_g, short_filter, med_filter, out_weight, head):
    half_width = D // 2
    length = query_g.shape[0]
    med_taps = jnp.repeat(med_filter.astype(jnp.float32), CPG, axis=1)
    feat_q = directed(query_g.astype(jnp.float32), short_filter[:, 0, :], False, False)
    feat_k = directed(key_g.astype(jnp.float32), short_filter[:, 1, :], False, False)
    feat_v = directed(value_g.astype(jnp.float32), short_filter[:, 2, :], False, False)
    gate = feat_q.astype(jnp.bfloat16)
    products = (feat_k * feat_v).astype(jnp.bfloat16)
    long_mix = directed(products.astype(jnp.float32), med_taps, False, True)
    gated = (gate.astype(jnp.float32) * long_mix).astype(jnp.bfloat16)
    gated_rows = jnp.concatenate([gated[:, :half_width], gated[:, half_width:]], axis=0)
    branch = jnp.dot(gated_rows, out_weight, preferred_element_type=jnp.float32)
    state = stream_g.astype(jnp.float32) + jnp.concatenate([branch[:length], branch[length:]], axis=1)
    flipped = head[::-1]
    logits = jnp.dot(state[:, :half_width], head.T, precision=lax.Precision.HIGHEST) + jnp.dot(
        state[:, half_width:], flipped.T, precision=lax.Precision.HIGHEST)
    exponent = jnp.exp(logits)
    softmax_out = exponent / jnp.sum(exponent, axis=1, keepdims=True)
    one_hot = (target_g[:, None] == jnp.arange(NUC, dtype=jnp.int32)[None, :]).astype(jnp.float32)
    logit_grad = loss_scale * (softmax_out - one_hot)
    state_grad = jnp.concatenate([
        jnp.dot(logit_grad, head, precision=lax.Precision.HIGHEST),
        jnp.dot(logit_grad, flipped, precision=lax.Precision.HIGHEST)], axis=1).astype(jnp.bfloat16)
    grad_rows = jnp.concatenate([state_grad[:, :half_width], state_grad[:, half_width:]], axis=0)
    gated_grad_rows = jnp.dot(grad_rows, out_weight.T, preferred_element_type=jnp.float32)
    gated_grad = jnp.concatenate([gated_grad_rows[:length], gated_grad_rows[length:]], axis=1)
    gate_grad = gated_grad * long_mix
    mix_grad = (gated_grad * gate.astype(jnp.float32)).astype(jnp.bfloat16)
    products_grad = directed(mix_grad.astype(jnp.float32), med_taps, True, True)
    key_feat_grad = products_grad * feat_v
    value_feat_grad = products_grad * feat_k
    query_out = directed(gate_grad, short_filter[:, 0, :], True, False).astype(jnp.bfloat16)
    key_out = directed(key_feat_grad, short_filter[:, 1, :], True, False).astype(jnp.bfloat16)
    value_out = directed(value_feat_grad, short_filter[:, 2, :], True, False).astype(jnp.bfloat16)
    weight_term = jnp.dot(gated_rows.T, grad_rows, preferred_element_type=jnp.float32)
    return query_out, key_out, value_out, weight_term


def reference(query, key, value, stream, targets, short_filter, med_filter, out_weight, head):
    def scan_step(carry, inputs):
        query_g, key_g, value_g, stream_g, target_g = inputs
        query_out, key_out, value_out, weight_term = one_genome(
            query_g, key_g, value_g, stream_g, target_g, short_filter, med_filter, out_weight, head)
        return carry + weight_term, (query_out, key_out, value_out)

    initial = jnp.zeros((D // 2, D // 2), jnp.float32)
    summed, grads = lax.scan(scan_step, initial, (query, key, value, stream, targets))
    return grads[0], grads[1], grads[2], summed / loss_scale
```

```python
import jax
import jax.numpy as jnp
import numpy as np
from jax import lax
from jax.sharding import PartitionSpec as P

loss_scale = 64.0
far = 136
near = 8
span = 296
window = 216
step = 80
keep = 88
lead = window - keep
freqs = 112


def dft_tables():
    omega = 2.0 * np.pi * (np.arange(freqs) + 0.5) / (2 * freqs)
    rows = np.arange(window)
    forward = np.concatenate([np.cos(omega[:, None] * rows), -np.sin(omega[:, None] * rows)])
    inverse = np.concatenate([np.cos(omega[:, None] * rows), -np.sin(omega[:, None] * rows)]).T / freqs
    return forward, inverse


def halves(table):
    upper = jnp.asarray(table, jnp.float32).astype(jnp.bfloat16)
    lower = (jnp.asarray(table, jnp.float32) - upper.astype(jnp.float32)).astype(jnp.bfloat16)
    return upper, lower


def long_conv(ext, spectrum, causal):
    forward, inverse = dft_tables()
    inverse = inverse[lead:] if causal else inverse[:keep]
    upper, lower = halves(forward)
    analysis = jnp.concatenate([upper, lower], axis=0)
    inv_upper, inv_lower = halves(inverse)
    synthesis = jnp.concatenate([inv_upper, inv_upper, inv_lower], axis=1)
    gain_re, gain_im = spectrum[:freqs], spectrum[freqs:]
    if not causal:
        gain_im = -gain_im
    pieces = []
    for index in range(2):
        both = jnp.dot(
            analysis, ext[index * step : index * step + window], preferred_element_type=jnp.float32
        )
        bins = both[: 2 * freqs] + both[2 * freqs :]
        re, im = bins[:freqs], bins[freqs:]
        mixed = jnp.concatenate([re * gain_re - im * gain_im, re * gain_im + im * gain_re], axis=0)
        high = mixed.astype(jnp.bfloat16)
        low = (mixed - high.astype(jnp.float32)).astype(jnp.bfloat16)
        pieces.append(
            jnp.dot(
                synthesis,
                jnp.concatenate([high, low, high], axis=0),
                preferred_element_type=jnp.float32,
            )
        )
    return jnp.concatenate([pieces[0][:step], pieces[1]], axis=0)


def taps(padded, filters, start, count, sign):
    total = None
    for offset in range(filters.shape[0]):
        begin = start - sign * offset
        term = filters[offset] * padded[begin : begin + count].astype(jnp.float32)
        total = term if total is None else total + term
    return total


def per_device(query, key, value, stream, targets, short_filter, med_filter, out_weight, head):
    length = query.shape[1]
    half = query.shape[2] // 2
    count = lax.axis_size("seq")
    rightward = [(i, i + 1) for i in range(count - 1)]
    leftward = [(i + 1, i) for i in range(count - 1)]
    query, key, value, stream = query[0], key[0], value[0], stream[0]
    highest = lax.Precision.HIGHEST

    weight_head = lax.dot_general(
        out_weight.astype(jnp.float32), head, (((1,), (1,)), ((), ())), precision=highest
    )
    weight_head = lax.all_gather(weight_head, "fsdp", axis=0, tiled=True)

    def lo(array, rows):
        return array[:rows]

    def hi(array, rows):
        return array[length - rows :]

    qf, kf, vf = query[:, :half], key[:, :half], value[:, :half]
    qr, kr, vr = query[:, half:], key[:, half:], value[:, half:]
    from_left = lax.ppermute(
        jnp.concatenate([hi(kf, far), hi(vf, far), hi(qf, near), hi(kr, near), hi(vr, near)], axis=0),
        "seq",
        rightward,
    )
    from_right = lax.ppermute(
        jnp.concatenate([lo(kr, far), lo(vr, far), lo(qr, near), lo(kf, near), lo(vf, near)], axis=0),
        "seq",
        leftward,
    )
    far_qr = lax.ppermute(hi(qr, far), "seq", rightward)
    far_qf = lax.ppermute(lo(qf, far), "seq", leftward)
    cuts = [far, 2 * far, 2 * far + near, 2 * far + 2 * near]
    left_kf, left_vf, left_qf, left_kr, left_vr = jnp.split(from_left, cuts, axis=0)
    right_kr, right_vr, right_qr, right_kf, right_vf = jnp.split(from_right, cuts, axis=0)

    wq, wk, wv = short_filter[:, 0], short_filter[:, 1], short_filter[:, 2]
    kf_feat = taps(jnp.concatenate([left_kf, kf, right_kf]), wk, near, span, 1)
    vf_feat = taps(jnp.concatenate([left_vf, vf, right_vf]), wv, near, span, 1)
    kr_feat = taps(jnp.concatenate([left_kr, kr, right_kr]), wk, 0, span, -1)
    vr_feat = taps(jnp.concatenate([left_vr, vr, right_vr]), wv, 0, span, -1)
    gate_f = taps(jnp.concatenate([left_qf, qf, far_qf]), wq, near, span, 1).astype(jnp.bfloat16)
    gate_r = taps(jnp.concatenate([far_qr, qr, right_qr]), wq, 0, span, -1).astype(jnp.bfloat16)

    forward, _ = dft_tables()
    med_taps, groups = med_filter.shape
    expand = np.arange(half)[None, :] // (half // groups) == np.arange(groups)[:, None]
    wide = jnp.dot(med_filter, jnp.asarray(expand, jnp.bfloat16))
    both = jnp.dot(
        jnp.concatenate(halves(forward[:, :med_taps]), axis=0),
        wide,
        preferred_element_type=jnp.float32,
    )
    spectrum = both[: 2 * freqs] + both[2 * freqs :]

    mix_f = long_conv((kf_feat * vf_feat).astype(jnp.bfloat16), spectrum, True)
    mix_r = long_conv((kr_feat * vr_feat).astype(jnp.bfloat16), spectrum, False)
    gated_f = (gate_f[:length].astype(jnp.float32) * mix_f[:length]).astype(jnp.bfloat16)
    gated_r = (gate_r[far:].astype(jnp.float32) * mix_r[near:]).astype(jnp.bfloat16)

    flipped = head[::-1]
    logits = (
        jnp.dot(gated_f.astype(jnp.float32), weight_head, precision=highest)
        + jnp.dot(gated_r.astype(jnp.float32), weight_head[:, ::-1], precision=highest)
        + jnp.dot(stream[:, :half].astype(jnp.float32), head.T, precision=highest)
        + jnp.dot(stream[:, half:].astype(jnp.float32), flipped.T, precision=highest)
    )
    exponent = jnp.exp(logits - jnp.max(logits, axis=1, keepdims=True))
    softmax_out = exponent / jnp.sum(exponent, axis=1, keepdims=True)
    one_hot = (
        targets[0][:, None] == jnp.arange(head.shape[0], dtype=jnp.int32)[None, :]
    ).astype(jnp.float32)
    logit_grad = loss_scale * (softmax_out - one_hot)

    left_grad = lax.ppermute(hi(logit_grad, far), "seq", rightward)
    right_grad = lax.ppermute(lo(logit_grad, far), "seq", leftward)

    partial = jnp.concatenate(
        [
            lax.dot_general(
                gated_f.astype(jnp.float32), logit_grad, (((0,), (0,)), ((), ())), precision=highest
            ),
            lax.dot_general(
                gated_r.astype(jnp.float32), logit_grad, (((0,), (0,)), ((), ())), precision=highest
            )[:, ::-1],
        ],
        axis=1,
    )
    partial = partial[:, :4] + partial[:, 4:]
    summed = lax.psum_scatter(lax.psum(partial, "seq"), "fsdp", scatter_dimension=0, tiled=True)
    out_grad = jnp.dot(summed, head, precision=highest) / loss_scale

    def outer(grad, reverse):
        table = weight_head.T[::-1] if reverse else weight_head.T
        total = grad[:, 0:1] * table[0]
        for index in range(1, 4):
            total = total + grad[:, index : index + 1] * table[index]
        return total

    gated_grad_f = outer(jnp.concatenate([logit_grad, right_grad]), False)
    gated_grad_r = outer(jnp.concatenate([left_grad, logit_grad]), True)
    mix_grad_f = (gated_grad_f * gate_f.astype(jnp.float32)).astype(jnp.bfloat16)
    mix_grad_r = (gated_grad_r * gate_r.astype(jnp.float32)).astype(jnp.bfloat16)
    back_f = long_conv(mix_grad_f, spectrum, False)
    back_r = long_conv(mix_grad_r, spectrum, True)
    rows = length + near
    query_grad = jnp.concatenate(
        [
            taps(gated_grad_f[:rows] * mix_f, wq, 0, length, -1),
            taps(gated_grad_r[far - near :] * mix_r, wq, near, length, 1),
        ],
        axis=1,
    )
    key_grad = jnp.concatenate(
        [
            taps(back_f * vf_feat[span - rows :], wk, 0, length, -1),
            taps(back_r * vr_feat[:rows], wk, near, length, 1),
        ],
        axis=1,
    )
    value_grad = jnp.concatenate(
        [
            taps(back_f * kf_feat[span - rows :], wv, 0, length, -1),
            taps(back_r * kr_feat[:rows], wv, near, length, 1),
        ],
        axis=1,
    )
    return tuple(g.astype(jnp.bfloat16)[None] for g in (query_grad, key_grad, value_grad)) + (
        out_grad,
    )


def solution(mesh):
    rows = P("fsdp", "seq", None)
    placed = (rows, rows, rows, rows, P("fsdp", "seq"), P(), P(), P("fsdp", None), P())
    return jax.shard_map(
        per_device,
        mesh=mesh,
        in_specs=placed,
        out_specs=(rows, rows, rows, P("fsdp", None)),
        check_vma=False,
    )
```

```python
import functools

import jax
import jax.numpy as jnp
import ml_dtypes
import numpy as np
from jax import lax
from jax.experimental import pallas as pl
from jax.experimental.pallas import tpu as pltpu
from jax.sharding import PartitionSpec as P

loss_scale = 64.0
far = 136
near = 8
span = 296
window = 216
step = 80
keep = 88
lead = window - keep
freqs = 112
bins = 2 * freqs
columns = 1024
per_group = 16
parts = 16
lanes = 128
sub = 256
vmem_limit = 24 * 1024 * 1024


def split_np(table):
    upper = table.astype(ml_dtypes.bfloat16)
    lower = (table - upper.astype(np.float64)).astype(ml_dtypes.bfloat16)
    return upper, lower


def dft_tables():
    omega = 2.0 * np.pi * (np.arange(freqs) + 0.5) / bins
    rows = np.arange(window)
    angles = omega[:, None] * rows
    forward = np.concatenate([np.cos(angles), -np.sin(angles)])
    return forward, forward.T / freqs


def split_bf16(value):
    upper = value.astype(jnp.bfloat16)
    return upper, (value - upper.astype(jnp.float32)).astype(jnp.bfloat16)


def dot(left, right):
    return jnp.dot(left, right, preferred_element_type=jnp.float32)


def dot_t(left, right):
    return lax.dot_general(
        left, right, (((1,), (1,)), ((), ())), preferred_element_type=jnp.float32
    )


def dot_ta(left, right):
    return lax.dot_general(
        left, right, (((0,), (0,)), ((), ())), preferred_element_type=jnp.float32
    )


def taps(pieces, weight, member, start, count, sign):
    rows = jnp.concatenate([piece.astype(jnp.float32) for piece in pieces], axis=0)
    total = rows.shape[0]
    tap = [weight[offset, member : member + 1, :] for offset in range(7)]

    def moved(value, by):
        return pltpu.roll(value, (sign * by) % total, 0)

    one = moved(rows, 1)
    two = moved(rows, 2)
    tail = tap[4] * rows + tap[5] * one + tap[6] * two
    tail = tap[2] * rows + tap[3] * one + moved(tail, 2)
    tail = tap[0] * rows + tap[1] * one + moved(tail, 2)
    return tail[start : start + count]


def gains(med, analysis, block):
    groups = med.shape[1]
    channel = lax.broadcasted_iota(jnp.int32, (groups, columns), 1) + block * columns
    group = lax.broadcasted_iota(jnp.int32, (groups, columns), 0)
    expand = jnp.where(channel // per_group == group, 1.0, 0.0).astype(jnp.bfloat16)
    wide = dot(med, expand).astype(jnp.bfloat16)
    count = med.shape[0]
    return dot(analysis[0, :, :count], wide) + dot(analysis[1, :, :count], wide)


def pack_kernel(
    length, q, k, v, out_weight, head,
    to_right, to_left, far_right, far_left, shard_out, head_out,
    sems,
):
    half = to_right.shape[1]
    copies = []

    def move(source, first, rows, side, target, at):
        copies.append(
            pltpu.make_async_copy(
                source.at[pl.ds(first, rows), pl.ds(side * half, half)],
                target.at[pl.ds(at, rows), :],
                sems.at[len(copies)],
            )
        )
        copies[-1].start()

    for target, mine, last in ((to_right, 0, True), (to_left, 1, False)):
        far_at = length - far if last else 0
        near_at = length - near if last else 0
        move(k, far_at, far, mine, target, 0)
        move(v, far_at, far, mine, target, far)
        move(q, near_at, near, mine, target, 2 * far)
        move(k, near_at, near, 1 - mine, target, 2 * far + near)
        move(v, near_at, near, 1 - mine, target, 2 * far + 2 * near)
    move(q, length - far, far, 1, far_right, 0)
    move(q, 0, far, 0, far_left, 0)

    def thirds(value):
        first, rest = split_bf16(value)
        second = (value - first.astype(jnp.float32)).astype(jnp.bfloat16)
        third = (value - first.astype(jnp.float32) - second.astype(jnp.float32)).astype(
            jnp.bfloat16
        )
        return jnp.concatenate(
            [
                first.astype(jnp.float32),
                second.astype(jnp.float32),
                third.astype(jnp.float32),
                jnp.zeros((parts - 12, value.shape[1]), jnp.float32),
            ],
            axis=0,
        ).astype(jnp.bfloat16)

    coded = thirds(head[...])
    head_out[...] = coded
    found = dot_t(coded, out_weight[...])
    shard = thirds(found[0:4] + found[4:8] + found[8:12])
    for device in range(shard_out.shape[0]):
        shard_out[device] = shard
    for copy in copies:
        copy.wait()


def class_block(class_rows):
    return jnp.concatenate([class_rows[piece] for piece in range(class_rows.shape[0])], axis=1)


def long_conv(rows_ref, spectrum, analysis, synthesis, causal):
    gain_re = spectrum[0:freqs, :]
    gain_im = spectrum[freqs:bins, :]
    if not causal:
        gain_im = -gain_im
    pieces = []
    for index in range(2):
        rows = rows_ref[index * step : index * step + window, :]
        found = dot(analysis[0], rows) + dot(analysis[1], rows)
        re, im = found[:freqs], found[freqs:]
        mixed = jnp.concatenate([re * gain_re - im * gain_im, re * gain_im + im * gain_re], axis=0)
        high, low = split_bf16(mixed)
        piece = dot(synthesis[0], high) + dot(synthesis[0], low) + dot(synthesis[1], high)
        pieces.append(piece[:step] if index == 0 else piece)
    return jnp.concatenate(pieces, axis=0)


def forward_kernel(
    length, q, k, v, s, left, right, weight, head_rows, class_rows, med, target, analysis,
    synth_c, synth_a, fold,
    gate_out, gated_out, mix_out, key_out, value_out, grad_out,
    products, spectrum, sums,
):
    block = pl.program_id(0)
    side = pl.program_id(1)

    @pl.when((block == 0) & (side == 0))
    def _():
        sums[...] = jnp.zeros_like(sums)

    @pl.when(side == 0)
    def _():
        spectrum[...] = gains(med[...], analysis, block)

    def one(forward):
        main, other = (left, right) if forward else (right, left)
        sign = 1 if forward else -1
        start = near if forward else 0
        first = span - length - near if forward else 0

        def order(*pieces):
            return pieces if forward else pieces[::-1]

        for at in range(0, columns, sub):
            cols = slice(at, at + sub)
            taken = weight[:, :, cols]
            k_far, v_far = main[0:far, cols], main[far : 2 * far, cols]
            q_near = main[2 * far : 2 * far + near, cols]
            k_near = other[2 * far + near : 2 * far + 2 * near, cols]
            v_near = other[2 * far + 2 * near : 2 * far + 3 * near, cols]
            key_feat = taps(order(k_far, k[:, cols], k_near), taken, 1, start, span, sign)
            key_out[:, cols] = key_feat[first : first + length + near].astype(jnp.bfloat16)
            value_feat = taps(order(v_far, v[:, cols], v_near), taken, 2, start, span, sign)
            value_out[:, cols] = value_feat[first : first + length + near].astype(jnp.bfloat16)
            products[:, cols] = (key_feat * value_feat).astype(jnp.bfloat16)
            gate = taps(order(q_near, q[:, cols]), taken, 0, start, length, sign)
            gate_out[:, cols] = gate.astype(jnp.bfloat16)
        mix = long_conv(products, spectrum, analysis, synth_c if forward else synth_a, forward)
        mix_out[...] = mix.astype(jnp.bfloat16)
        local = mix[:length] if forward else mix[near:]
        gated = (gate_out[...].astype(jnp.float32) * local).astype(jnp.bfloat16)
        gated_out[...] = gated
        sums[0 if forward else 1] += dot_t(gated, class_block(class_rows)) + dot_t(
            s[...], head_rows[...]
        )

    pl.when(side == 0)(functools.partial(one, True))
    pl.when(side == 1)(functools.partial(one, False))

    @pl.when((block == pl.num_programs(0) - 1) & (side == 1))
    def _():
        exact = lax.Precision.HIGHEST
        logits = jnp.dot(
            sums[0], fold[0], precision=exact, preferred_element_type=jnp.float32
        ) + jnp.dot(sums[1], fold[1], precision=exact, preferred_element_type=jnp.float32)
        logits = jnp.transpose(logits)[:8]
        row = lax.broadcasted_iota(jnp.int32, logits.shape, 0)
        valid = row < 4
        top = jnp.max(jnp.where(valid, logits, -jnp.inf), axis=0, keepdims=True)
        exponent = jnp.where(valid, jnp.exp(logits - top), 0.0)
        softmax_out = exponent / jnp.sum(exponent, axis=0, keepdims=True)
        one_hot = jnp.where(row == target[...], 1.0, 0.0)
        grad_out[...] = loss_scale * (softmax_out - one_hot)


def middle_kernel(
    length, q, far_left, far_right, gated, weight, grad,
    partial_out, halo_out,
    turned,
):
    block = pl.program_id(0)
    side = pl.program_id(1)

    @pl.when((block == 0) & (side == 0))
    def _():
        turned[0] = grad[...]
        for lane in range(4):
            turned[1, lane : lane + 1, :] = grad[3 - lane : 4 - lane, :]
        turned[1, 4:8, :] = jnp.zeros((4, length), jnp.float32)

    def one(forward):
        high, low = split_bf16(turned[0 if forward else 1])
        term = dot(high, gated[...]) + dot(low, gated[...])
        for piece in range(columns // 128):
            cut = term[:, piece * 128 : piece * 128 + 128]
            if forward:
                partial_out[piece] = cut
            else:
                partial_out[piece] += cut
        for at in range(0, columns, sub):
            cols = slice(at, at + sub)
            taken = weight[:, :, cols]
            if forward:
                halo = taps(
                    (q[length - near :, cols], far_right[:, cols]), taken, 0, near, far, 1
                )
            else:
                halo = taps((far_left[:, cols], q[:near, cols]), taken, 0, 0, far, -1)
            halo_out[:, cols] = halo.astype(jnp.bfloat16)

    pl.when(side == 0)(functools.partial(one, True))
    pl.when(side == 1)(functools.partial(one, False))


def backward_kernel(
    length, gate, halo, mix, key_feat, value_feat, weight, class_rows, med, grad, grad_left,
    grad_right, analysis, synth_c, synth_a, place,
    query_out, key_out, value_out,
    coded, mix_grad, spectrum,
):
    block = pl.program_id(0)
    side = pl.program_id(1)
    extent = length + near

    @pl.when((block == 0) & (side == 0))
    def _():
        def code(piece, side_at):
            high, low = split_bf16(piece[...])
            return (
                dot_ta(high, place[side_at, 0]) + dot_ta(low, place[side_at, 1])
            ).astype(jnp.bfloat16)

        coded[0, :length] = code(grad, 0)
        coded[0, length:] = code(grad_right, 0)[:far]
        coded[1, :far] = code(grad_left, 1)[length - far :]
        coded[1, far:] = code(grad, 1)

    @pl.when(side == 0)
    def _():
        spectrum[...] = gains(med[...], analysis, block)

    def one(forward):
        classes = class_block(class_rows)
        grads = dot(coded[0 if forward else 1], jnp.concatenate([classes, classes], axis=0))
        start = 0 if forward else near
        sign = -1 if forward else 1
        gates = (gate[...], halo[...]) if forward else (halo[...], gate[...])
        gates = jnp.concatenate([piece.astype(jnp.float32) for piece in gates], axis=0)
        mix_grad[...] = (grads * gates).astype(jnp.bfloat16)
        near_grads = grads[:extent] if forward else grads[span - extent :]
        for at in range(0, columns, sub):
            cols = slice(at, at + sub)
            query_out[:, cols] = taps(
                (near_grads[:, cols] * mix[:, cols].astype(jnp.float32),),
                weight[:, :, cols], 0, start, length, sign,
            ).astype(jnp.bfloat16)
        back = long_conv(
            mix_grad, spectrum, analysis, synth_a if forward else synth_c, not forward
        )
        for at in range(0, columns, sub):
            cols = slice(at, at + sub)
            for member, feat, out in ((1, value_feat, key_out), (2, key_feat, value_out)):
                out[:, cols] = taps(
                    (back[:, cols] * feat[:, cols].astype(jnp.float32),),
                    weight[:, :, cols], member, start, length, sign,
                ).astype(jnp.bfloat16)

    pl.when(side == 0)(functools.partial(one, True))
    pl.when(side == 1)(functools.partial(one, False))


def final_kernel(terms, head, out):
    total = jnp.sum(terms[...], axis=0)
    out[...] = lax.dot_general(
        total[:4],
        head[...] * (1.0 / loss_scale),
        (((0,), (0,)), ((), ())),
        precision=lax.Precision.HIGHEST,
        preferred_element_type=jnp.float32,
    )


def per_device(query, key, value, stream, targets, short_filter, med_filter, out_weight, head):
    length = query.shape[1]
    channels = query.shape[2]
    half = channels // 2
    blocks = half // columns
    count = lax.axis_size("seq")
    owners = lax.axis_size("fsdp")
    own = half // owners
    rightward = [(i, i + 1) for i in range(count - 1)]
    leftward = [(i + 1, i) for i in range(count - 1)]
    query, key, value, stream = query[0], key[0], value[0], stream[0]
    bf16, f32 = jnp.bfloat16, jnp.float32
    extent = length + near
    packed = 2 * far + 3 * near
    shape = jax.ShapeDtypeStruct
    raw = pl.BlockSpec(memory_space=pl.ANY)
    whole = pl.BlockSpec(memory_space=pltpu.VMEM)
    limit = pltpu.CompilerParams(vmem_limit_bytes=vmem_limit)

    to_right, to_left, far_right, far_left, shard, head_rows = pl.pallas_call(
        functools.partial(pack_kernel, length),
        in_specs=[raw] * 3 + [whole] * 2,
        out_specs=[raw] * 4 + [whole] * 2,
        out_shape=[shape((packed, half), bf16)] * 2
        + [shape((far, half), bf16)] * 2
        + [shape((owners, parts, own), bf16), shape((parts, half), bf16)],
        scratch_shapes=[pltpu.SemaphoreType.DMA((12,))],
        compiler_params=limit,
        name="pack",
    )(query, key, value, out_weight, head)

    from_left = lax.ppermute(to_right, "seq", rightward)
    from_right = lax.ppermute(to_left, "seq", leftward)
    class_rows = lax.all_to_all(shard, "fsdp", 0, 0, tiled=True)
    if own != lanes:
        class_rows = class_rows.reshape(owners, parts, -1, lanes).transpose(0, 2, 1, 3)
        class_rows = class_rows.reshape(-1, parts, lanes)
    halo_left = lax.ppermute(far_right, "seq", rightward)
    halo_right = lax.ppermute(far_left, "seq", leftward)

    forward, inverse = dft_tables()
    analysis = jnp.asarray(np.stack(split_np(forward)))
    synth_c = jnp.asarray(np.stack(split_np(inverse[lead:])))
    synth_a = jnp.asarray(np.stack(split_np(inverse[:keep])))

    fold = np.zeros((2, parts, 128), np.float32)
    place = np.zeros((2, 2, 8, 2 * parts), np.float32)
    for lane in range(4):
        for part in range(3):
            fold[0, 4 * part + lane, lane] = 1.0
            fold[1, 4 * part + 3 - lane, lane] = 1.0
            for level in range(2):
                place[0, level, lane, level * parts + 4 * part + lane] = 1.0
                place[1, level, 3 - lane, level * parts + 4 * part + lane] = 1.0
    place = jnp.asarray(place.astype(ml_dtypes.bfloat16))

    def full(array):
        rank = len(array.shape)
        return pl.BlockSpec(array.shape, lambda *_: (0,) * rank)

    def by_channel(rows):
        return pl.BlockSpec((rows, columns), lambda b, s: (0, s * blocks + b))

    def by_half(rows):
        return pl.BlockSpec((rows, columns), lambda b, s: (0, b))

    weight_spec = pl.BlockSpec(
        short_filter.shape[:2] + (columns,), lambda b, s: (0, 0, b)
    )

    def by_owner(rows):
        return pl.BlockSpec((columns // lanes, rows, lanes), lambda b, s: (b, 0, 0))

    params = pltpu.CompilerParams(
        dimension_semantics=("arbitrary", "arbitrary"), vmem_limit_bytes=vmem_limit
    )
    grad_shape = shape((8, length), f32)
    gate, gated, mix, key_feat, value_feat, grad = pl.pallas_call(
        functools.partial(forward_kernel, length),
        grid=(blocks, 2),
        in_specs=[by_channel(length)] * 4
        + [by_half(packed)] * 2
        + [
            weight_spec, by_half(parts), by_owner(parts), full(med_filter), full(targets),
            full(analysis), full(synth_c), full(synth_a), full(fold),
        ],
        out_specs=[by_channel(length)] * 2 + [by_channel(extent)] * 3 + [full(grad_shape)],
        out_shape=[shape((length, channels), bf16)] * 2
        + [shape((extent, channels), bf16)] * 3
        + [grad_shape],
        scratch_shapes=[
            pltpu.VMEM((span, columns), bf16),
            pltpu.VMEM((bins, columns), f32),
            pltpu.VMEM((2, length, parts), f32),
        ],
        compiler_params=params,
        name="features_and_logits",
    )(
        query, key, value, stream, from_left, from_right, short_filter, head_rows, class_rows,
        med_filter, targets, analysis, synth_c, synth_a, jnp.asarray(fold),
    )

    grad_left = lax.ppermute(grad, "seq", rightward)
    grad_right = lax.ppermute(grad, "seq", leftward)

    partial, halo = pl.pallas_call(
        functools.partial(middle_kernel, length),
        grid=(blocks, 2),
        in_specs=[
            by_channel(length), by_half(far), by_half(far), by_channel(length), weight_spec,
            full(grad),
        ],
        out_specs=[by_owner(8), by_channel(far)],
        out_shape=[shape((half // lanes, 8, lanes), f32), shape((far, channels), bf16)],
        scratch_shapes=[pltpu.VMEM((2, 8, length), f32)],
        compiler_params=params,
        name="weight_partial_and_gate_halo",
    )(query, halo_left, halo_right, gated, short_filter, grad)

    query_grad, key_grad, value_grad = pl.pallas_call(
        functools.partial(backward_kernel, length),
        grid=(blocks, 2),
        in_specs=[by_channel(length), by_channel(far)]
        + [by_channel(extent)] * 3
        + [
            weight_spec, by_owner(parts), full(med_filter), full(grad), full(grad), full(grad),
            full(analysis), full(synth_c), full(synth_a), full(place),
        ],
        out_specs=[by_channel(length)] * 3,
        out_shape=[shape((length, channels), bf16)] * 3,
        scratch_shapes=[
            pltpu.VMEM((2, span, 2 * parts), bf16),
            pltpu.VMEM((span, columns), bf16),
            pltpu.VMEM((bins, columns), f32),
        ],
        compiler_params=params,
        name="gradients",
    )(
        gate, halo, mix, key_feat, value_feat, short_filter, class_rows, med_filter, grad,
        grad_left, grad_right, analysis, synth_c, synth_a, place,
    )

    if own != lanes:
        partial = partial.reshape(owners, -1, 8, lanes).transpose(0, 2, 1, 3)
        partial = partial.reshape(owners, 8, own)
    over_genomes = jnp.sum(lax.all_to_all(partial, "fsdp", 0, 0, tiled=True), axis=0)
    spread = jnp.broadcast_to(over_genomes, (count,) + over_genomes.shape)
    terms = lax.all_to_all(spread, "seq", 0, 0, tiled=True)
    out_grad = pl.pallas_call(
        final_kernel,
        in_specs=[whole] * 2,
        out_specs=whole,
        out_shape=shape((own, half), f32),
        compiler_params=limit,
        name="final",
    )(terms, head)
    return query_grad[None], key_grad[None], value_grad[None], out_grad


def solution(mesh):
    rows = P("fsdp", "seq", None)
    placed = (rows, rows, rows, rows, P("fsdp", "seq"), P(), P(), P("fsdp", None), P())
    return jax.shard_map(
        per_device,
        mesh=mesh,
        in_specs=placed,
        out_specs=(rows, rows, rows, P("fsdp", None)),
        check_vma=False,
    )
```

```python
import functools

import jax
import jax.numpy as jnp
import ml_dtypes
import numpy as np
from jax import lax
from jax.experimental import pallas as pl
from jax.experimental.pallas import tpu as pltpu
from jax.sharding import PartitionSpec as P

loss_scale = 64.0
far = 136
near = 8
span = 296
window = 216
step = 80
keep = 88
lead = window - keep
freqs = 112
bins = 2 * freqs
columns = 1024
per_group = 16
parts = 16
lanes = 128
sub = 256
vmem_limit = 34 * 1024 * 1024


def split_np(table):
    upper = table.astype(ml_dtypes.bfloat16)
    lower = (table - upper.astype(np.float64)).astype(ml_dtypes.bfloat16)
    return upper, lower


def dft_tables():
    omega = 2.0 * np.pi * (np.arange(freqs) + 0.5) / bins
    rows = np.arange(window)
    angles = omega[:, None] * rows
    forward = np.concatenate([np.cos(angles), -np.sin(angles)])
    return forward, forward.T / freqs


def split_bf16(value):
    upper = value.astype(jnp.bfloat16)
    return upper, (value - upper.astype(jnp.float32)).astype(jnp.bfloat16)


def dot(left, right):
    return jnp.dot(left, right, preferred_element_type=jnp.float32)


def dot_t(left, right):
    return lax.dot_general(
        left, right, (((1,), (1,)), ((), ())), preferred_element_type=jnp.float32
    )


def dot_ta(left, right):
    return lax.dot_general(
        left, right, (((0,), (0,)), ((), ())), preferred_element_type=jnp.float32
    )


def taps(pieces, weight, member, start, count, sign):
    rows = jnp.concatenate([piece.astype(jnp.float32) for piece in pieces], axis=0)
    total = rows.shape[0]
    tap = [weight[offset, member : member + 1, :] for offset in range(7)]

    def moved(value, by):
        return pltpu.roll(value, (sign * by) % total, 0)

    one = moved(rows, 1)
    two = moved(rows, 2)
    tail = tap[4] * rows + tap[5] * one + tap[6] * two
    tail = tap[2] * rows + tap[3] * one + moved(tail, 2)
    tail = tap[0] * rows + tap[1] * one + moved(tail, 2)
    return tail[start : start + count]


def gains(med, analysis, block):
    groups = med.shape[1]
    channel = lax.broadcasted_iota(jnp.int32, (groups, columns), 1) + block * columns
    group = lax.broadcasted_iota(jnp.int32, (groups, columns), 0)
    expand = jnp.where(channel // per_group == group, 1.0, 0.0).astype(jnp.bfloat16)
    wide = dot(med, expand).astype(jnp.bfloat16)
    count = med.shape[0]
    both = dot(analysis[:, :count], wide)
    return both[:bins] + both[bins:]


def in_hbm(array):
    return pltpu.with_memory_space_constraint(array, pltpu.HBM)


def pack_kernel(
    length, q, k, v, out_weight, head,
    to_right, to_left, shard_out, head_out,
    sems, weight_sem, head_sem, weight_rows, head_values,
):
    half = to_right.shape[1]
    weight_copy = pltpu.make_async_copy(out_weight, weight_rows, weight_sem)
    weight_copy.start()
    head_copy = pltpu.make_async_copy(head, head_values, head_sem)
    head_copy.start()
    copies = []

    def move(source, first, rows, side, target, at):
        copies.append(
            pltpu.make_async_copy(
                source.at[pl.ds(first, rows), pl.ds(side * half, half)],
                target.at[pl.ds(at, rows), :],
                sems.at[len(copies)],
            )
        )
        copies[-1].start()

    for target, mine, last in ((to_right, 0, True), (to_left, 1, False)):
        far_at = length - far if last else 0
        near_at = length - near if last else 0
        move(k, far_at, far, mine, target, 0)
        move(v, far_at, far, mine, target, far)
        move(q, near_at, near, mine, target, 2 * far)
        move(k, near_at, near, 1 - mine, target, 2 * far + near)
        move(v, near_at, near, 1 - mine, target, 2 * far + 2 * near)

    def thirds(value):
        first, rest = split_bf16(value)
        second = (value - first.astype(jnp.float32)).astype(jnp.bfloat16)
        third = (value - first.astype(jnp.float32) - second.astype(jnp.float32)).astype(
            jnp.bfloat16
        )
        return jnp.concatenate(
            [
                first.astype(jnp.float32),
                second.astype(jnp.float32),
                third.astype(jnp.float32),
                jnp.zeros((parts - 12, value.shape[1]), jnp.float32),
            ],
            axis=0,
        ).astype(jnp.bfloat16)

    head_copy.wait()
    coded = thirds(head_values[...])
    head_out[...] = coded
    weight_copy.wait()
    found = dot_t(coded, weight_rows[...])
    shard = thirds(found[0:4] + found[4:8] + found[8:12])
    for device in range(shard_out.shape[0]):
        shard_out[device] = shard
    for copy in copies:
        copy.wait()


def class_block(class_rows):
    return jnp.concatenate([class_rows[piece] for piece in range(class_rows.shape[0])], axis=1)


def long_conv(rows_ref, spectrum, analysis, synthesis, causal):
    gain_re = spectrum[0:freqs, :]
    gain_im = spectrum[freqs:bins, :]
    if not causal:
        gain_im = -gain_im
    pieces = []
    for index in range(2):
        both = dot(analysis[...], rows_ref[index * step : index * step + window, :])
        re = both[:freqs] + both[bins : bins + freqs]
        im = both[freqs:bins] + both[bins + freqs :]
        mixed = jnp.concatenate([re * gain_re - im * gain_im, re * gain_im + im * gain_re], axis=0)
        high, low = split_bf16(mixed)
        both = dot(synthesis[...], high)
        piece = both[:keep] + both[keep:] + dot(synthesis[:keep], low)
        pieces.append(piece[:step] if index == 0 else piece)
    return jnp.concatenate(pieces, axis=0)


def kept(flag, piece):
    return jnp.where(flag, piece, jnp.zeros_like(piece))


def forward_kernel(
    length, inner, q, k, v, s, left, right, weight, head_rows, class_rows, med, target, analysis,
    synth_c, synth_a, fold,
    gate_out, gated_out, mix_out, key_out, value_out, grad_out,
    products, spectrum, sums,
):
    block = pl.program_id(0)
    side = pl.program_id(1)

    @pl.when((block == 0) & (side == 0))
    def _():
        sums[...] = jnp.zeros_like(sums)

    @pl.when(side == 0)
    def _():
        spectrum[...] = gains(med[...], analysis, block)

    def one(forward):
        main, other = (left, right) if forward else (right, left)
        main_flag, other_flag = (inner[0] > 0, inner[1] > 0) if forward else (
            inner[1] > 0, inner[0] > 0,
        )
        sign = 1 if forward else -1
        start = near if forward else 0
        first = span - length - near if forward else 0

        def order(*pieces):
            return pieces if forward else pieces[::-1]

        for at in range(0, columns, sub):
            cols = slice(at, at + sub)
            taken = weight[:, :, cols]
            k_far = kept(main_flag, main[0:far, cols].astype(jnp.float32))
            v_far = kept(main_flag, main[far : 2 * far, cols].astype(jnp.float32))
            q_near = main[2 * far : 2 * far + near, cols].astype(jnp.float32)
            q_near = kept(main_flag, q_near)
            k_near = other[2 * far + near : 2 * far + 2 * near, cols].astype(jnp.float32)
            k_near = kept(other_flag, k_near)
            v_near = other[2 * far + 2 * near : 2 * far + 3 * near, cols].astype(jnp.float32)
            v_near = kept(other_flag, v_near)
            key_feat = taps(order(k_far, k[:, cols], k_near), taken, 1, start, span, sign)
            key_out[:, cols] = key_feat[first : first + length + near].astype(jnp.bfloat16)
            value_feat = taps(order(v_far, v[:, cols], v_near), taken, 2, start, span, sign)
            value_out[:, cols] = value_feat[first : first + length + near].astype(jnp.bfloat16)
            products[:, cols] = (key_feat * value_feat).astype(jnp.bfloat16)
            gate = taps(order(q_near, q[:, cols]), taken, 0, start, length, sign)
            gate_out[:, cols] = gate.astype(jnp.bfloat16)
        mix = long_conv(products, spectrum, analysis, synth_c if forward else synth_a, forward)
        local = mix[:length] if forward else mix[near:]
        mix_out[...] = local.astype(jnp.bfloat16)
        gated = (gate_out[...].astype(jnp.float32) * local).astype(jnp.bfloat16)
        gated_out[...] = gated
        sums[0 if forward else 1] += dot_t(gated, class_block(class_rows)) + dot_t(
            s[...], head_rows[...]
        )

    pl.when(side == 0)(functools.partial(one, True))
    pl.when(side == 1)(functools.partial(one, False))

    @pl.when((block == pl.num_programs(0) - 1) & (side == 1))
    def _():
        exact = lax.Precision.HIGHEST
        logits = jnp.dot(
            sums[0], fold[0], precision=exact, preferred_element_type=jnp.float32
        ) + jnp.dot(sums[1], fold[1], precision=exact, preferred_element_type=jnp.float32)
        logits = jnp.transpose(logits)[:8]
        row = lax.broadcasted_iota(jnp.int32, logits.shape, 0)
        valid = row < 4
        top = jnp.max(jnp.where(valid, logits, -jnp.inf), axis=0, keepdims=True)
        exponent = jnp.where(valid, jnp.exp(logits - top), 0.0)
        softmax_out = exponent / jnp.sum(exponent, axis=0, keepdims=True)
        one_hot = jnp.where(row == target[...], 1.0, 0.0)
        grad_out[...] = loss_scale * (softmax_out - one_hot)


def middle_kernel(
    length, gate, gated, mix, class_rows, grad, place,
    partial_out, mix_grad_out, gate_grad_out, to_left, to_right,
    turned, coded,
):
    block = pl.program_id(0)
    side = pl.program_id(1)

    @pl.when((block == 0) & (side == 0))
    def _():
        high, low = split_bf16(grad[...])
        for side_at in range(2):
            coded[side_at] = (
                dot_ta(high, place[side_at, 0]) + dot_ta(low, place[side_at, 1])
            ).astype(jnp.bfloat16)
        turned[0] = grad[...]
        for lane in range(4):
            turned[1, lane : lane + 1, :] = grad[3 - lane : 4 - lane, :]
        turned[1, 4:8, :] = jnp.zeros((4, length), jnp.float32)

    def one(forward):
        high, low = split_bf16(turned[0 if forward else 1])
        term = dot(high, gated[...]) + dot(low, gated[...])
        for piece in range(columns // lanes):
            cut = term[:, piece * lanes : piece * lanes + lanes]
            if forward:
                partial_out[piece] = cut
            else:
                partial_out[piece] += cut
        classes = class_block(class_rows)
        grads = dot(coded[0 if forward else 1], jnp.concatenate([classes, classes], axis=0))
        mix_grad = (grads * gate[...].astype(jnp.float32)).astype(jnp.bfloat16)
        gate_grad = (grads * mix[...].astype(jnp.float32)).astype(jnp.bfloat16)
        mix_grad_out[...] = mix_grad
        gate_grad_out[...] = gate_grad
        if forward:
            to_left[0:far, :] = mix_grad[:far]
            to_left[far:, :] = gate_grad[:near]
        else:
            to_right[0:far, :] = mix_grad[length - far :]
            to_right[far:, :] = gate_grad[length - near :]

    pl.when(side == 0)(functools.partial(one, True))
    pl.when(side == 1)(functools.partial(one, False))


def backward_kernel(
    length, inner, mix_grad, gate_grad, left, right, key_feat, value_feat, weight, med, analysis,
    synth_c, synth_a,
    query_out, key_out, value_out,
    extended, spectrum,
):
    block = pl.program_id(0)
    side = pl.program_id(1)

    @pl.when(side == 0)
    def _():
        spectrum[...] = gains(med[...], analysis, block)

    def one(forward):
        halo = right if forward else left
        flag = (inner[1] if forward else inner[0]) > 0
        start = 0 if forward else near
        sign = -1 if forward else 1
        far_rows = kept(flag, halo[0:far, :].astype(jnp.float32)).astype(jnp.bfloat16)
        if forward:
            extended[0:length, :] = mix_grad[...]
            extended[length:, :] = far_rows
        else:
            extended[0:far, :] = far_rows
            extended[far:, :] = mix_grad[...]
        for at in range(0, columns, sub):
            cols = slice(at, at + sub)
            rim = kept(flag, halo[far:, cols].astype(jnp.float32))
            pieces = (gate_grad[:, cols], rim) if forward else (rim, gate_grad[:, cols])
            query_out[:, cols] = taps(
                pieces, weight[:, :, cols], 0, start, length, sign
            ).astype(jnp.bfloat16)
        back = long_conv(
            extended, spectrum, analysis, synth_a if forward else synth_c, not forward
        )
        for at in range(0, columns, sub):
            cols = slice(at, at + sub)
            for member, feat, out in ((1, value_feat, key_out), (2, key_feat, value_out)):
                out[:, cols] = taps(
                    (back[:, cols] * feat[:, cols].astype(jnp.float32),),
                    weight[:, :, cols], member, start, length, sign,
                ).astype(jnp.bfloat16)

    pl.when(side == 0)(functools.partial(one, True))
    pl.when(side == 1)(functools.partial(one, False))


def final_kernel(terms, head, out):
    total = jnp.sum(terms[...], axis=0)
    out[...] = lax.dot_general(
        total[:4],
        head[...] * (1.0 / loss_scale),
        (((0,), (0,)), ((), ())),
        precision=lax.Precision.HIGHEST,
        preferred_element_type=jnp.float32,
    )


def per_device(query, key, value, stream, targets, short_filter, med_filter, out_weight, head):
    length = query.shape[1]
    channels = query.shape[2]
    half = channels // 2
    blocks = half // columns
    count = lax.axis_size("seq")
    owners = lax.axis_size("fsdp")
    own = half // owners
    rightward = [(i, (i + 1) % count) for i in range(count)]
    leftward = [((i + 1) % count, i) for i in range(count)]
    query, key, value, stream = query[0], key[0], value[0], stream[0]
    bf16, f32 = jnp.bfloat16, jnp.float32
    extent = length + near
    packed = 2 * far + 3 * near
    shape = jax.ShapeDtypeStruct
    raw = pl.BlockSpec(memory_space=pltpu.HBM)
    whole = pl.BlockSpec(memory_space=pltpu.VMEM)
    scalars = pl.BlockSpec(memory_space=pltpu.SMEM)
    query, key, value, stream = in_hbm(query), in_hbm(key), in_hbm(value), in_hbm(stream)
    limit = pltpu.CompilerParams(vmem_limit_bytes=vmem_limit)

    to_right, to_left, shard, head_rows = pl.pallas_call(
        functools.partial(pack_kernel, length),
        in_specs=[raw] * 5,
        out_specs=[whole] * 4,
        out_shape=[shape((packed, half), bf16)] * 2
        + [shape((owners, parts, own), bf16), shape((parts, half), bf16)],
        scratch_shapes=[
            pltpu.SemaphoreType.DMA((10,)),
            pltpu.SemaphoreType.DMA,
            pltpu.SemaphoreType.DMA,
            pltpu.VMEM(out_weight.shape, bf16),
            pltpu.VMEM(head.shape, f32),
        ],
        compiler_params=limit,
        name="pack",
    )(query, key, value, out_weight, head)

    from_left = lax.ppermute(to_right, "seq", rightward)
    from_right = lax.ppermute(to_left, "seq", leftward)
    class_rows = lax.all_to_all(shard, "fsdp", 0, 0, tiled=True)
    if own != lanes:
        class_rows = class_rows.reshape(owners, parts, -1, lanes).transpose(0, 2, 1, 3)
        class_rows = class_rows.reshape(-1, parts, lanes)
    position = lax.axis_index("seq")
    inner = jnp.stack([position > 0, position < count - 1]).astype(jnp.int32)

    forward, inverse = dft_tables()
    analysis = jnp.asarray(np.concatenate(split_np(forward)))
    synth_c = jnp.asarray(np.concatenate(split_np(inverse[lead:])))
    synth_a = jnp.asarray(np.concatenate(split_np(inverse[:keep])))

    fold = np.zeros((2, parts, 128), np.float32)
    place = np.zeros((2, 2, 8, 2 * parts), np.float32)
    for lane in range(4):
        for part in range(3):
            fold[0, 4 * part + lane, lane] = 1.0
            fold[1, 4 * part + 3 - lane, lane] = 1.0
            for level in range(2):
                place[0, level, lane, level * parts + 4 * part + lane] = 1.0
                place[1, level, 3 - lane, level * parts + 4 * part + lane] = 1.0
    place = jnp.asarray(place.astype(ml_dtypes.bfloat16))

    def full(array):
        rank = len(array.shape)
        return pl.BlockSpec(array.shape, lambda *_: (0,) * rank)

    def by_channel(rows):
        return pl.BlockSpec((rows, columns), lambda b, s: (0, s * blocks + b))

    def by_half(rows):
        return pl.BlockSpec((rows, columns), lambda b, s: (0, b))

    weight_spec = pl.BlockSpec(
        short_filter.shape[:2] + (columns,), lambda b, s: (0, 0, b)
    )

    def by_owner(rows):
        return pl.BlockSpec((columns // lanes, rows, lanes), lambda b, s: (b, 0, 0))

    params = pltpu.CompilerParams(
        dimension_semantics=("arbitrary", "arbitrary"), vmem_limit_bytes=vmem_limit
    )
    grad_shape = shape((8, length), f32)
    gate, gated, mix, key_feat, value_feat, grad = pl.pallas_call(
        functools.partial(forward_kernel, length),
        grid=(blocks, 2),
        in_specs=[scalars]
        + [by_channel(length)] * 4
        + [by_half(packed)] * 2
        + [
            weight_spec, by_half(parts), by_owner(parts), full(med_filter), full(targets),
            full(analysis), full(synth_c), full(synth_a), full(fold),
        ],
        out_specs=[by_channel(length)] * 3 + [by_channel(extent)] * 2 + [full(grad_shape)],
        out_shape=[shape((length, channels), bf16)] * 3
        + [shape((extent, channels), bf16)] * 2
        + [grad_shape],
        scratch_shapes=[
            pltpu.VMEM((span, columns), bf16),
            pltpu.VMEM((bins, columns), f32),
            pltpu.VMEM((2, length, parts), f32),
        ],
        compiler_params=params,
        name="features_and_logits",
    )(
        inner, query, key, value, stream, from_left, from_right, short_filter, head_rows, class_rows,
        med_filter, targets, analysis, synth_c, synth_a, jnp.asarray(fold),
    )

    partial, mix_grad, gate_grad, to_left, to_right = pl.pallas_call(
        functools.partial(middle_kernel, length),
        grid=(blocks, 2),
        in_specs=[by_channel(length)] * 3 + [by_owner(parts), full(grad), full(place)],
        out_specs=[by_owner(8)] + [by_channel(length)] * 2 + [by_half(far + near)] * 2,
        out_shape=[shape((half // lanes, 8, lanes), f32)]
        + [shape((length, channels), bf16)] * 2
        + [shape((far + near, half), bf16)] * 2,
        scratch_shapes=[
            pltpu.VMEM((2, 8, length), f32),
            pltpu.VMEM((2, length, 2 * parts), bf16),
        ],
        compiler_params=params,
        name="weight_partial_and_mix_grad",
    )(gate, gated, mix, class_rows, grad, place)

    mix_grad, gate_grad = in_hbm(mix_grad), in_hbm(gate_grad)
    key_feat, value_feat = in_hbm(key_feat), in_hbm(value_feat)
    grad_left = lax.ppermute(to_right, "seq", rightward)
    grad_right = lax.ppermute(to_left, "seq", leftward)

    query_grad, key_grad, value_grad = pl.pallas_call(
        functools.partial(backward_kernel, length),
        grid=(blocks, 2),
        in_specs=[scalars]
        + [by_channel(length)] * 2
        + [by_half(far + near)] * 2
        + [by_channel(extent)] * 2
        + [weight_spec, full(med_filter), full(analysis), full(synth_c), full(synth_a)],
        out_specs=[by_channel(length)] * 3,
        out_shape=[shape((length, channels), bf16)] * 3,
        scratch_shapes=[pltpu.VMEM((span, columns), bf16), pltpu.VMEM((bins, columns), f32)],
        compiler_params=params,
        name="gradients",
    )(
        inner, mix_grad, gate_grad, grad_left, grad_right, key_feat, value_feat, short_filter,
        med_filter, analysis, synth_c, synth_a,
    )

    if own != lanes:
        partial = partial.reshape(owners, -1, 8, lanes).transpose(0, 2, 1, 3)
        partial = partial.reshape(owners, 8, own)
    over_genomes = jnp.sum(lax.all_to_all(partial, "fsdp", 0, 0, tiled=True), axis=0)
    spread = jnp.broadcast_to(over_genomes, (count,) + over_genomes.shape)
    terms = lax.all_to_all(spread, "seq", 0, 0, tiled=True)
    out_grad = pl.pallas_call(
        final_kernel,
        in_specs=[whole] * 2,
        out_specs=whole,
        out_shape=shape((own, half), f32),
        compiler_params=limit,
        name="final",
    )(terms, head)
    return query_grad[None], key_grad[None], value_grad[None], out_grad


def solution(mesh):
    rows = P("fsdp", "seq", None)
    placed = (rows, rows, rows, rows, P("fsdp", "seq"), P(), P(), P("fsdp", None), P())
    return jax.shard_map(
        per_device,
        mesh=mesh,
        in_specs=placed,
        out_specs=(rows, rows, rows, P("fsdp", None)),
        check_vma=False,
    )
```

```python
import functools

import jax
import jax.numpy as jnp
import ml_dtypes
import numpy as np
from jax import lax
from jax.experimental import pallas as pl
from jax.experimental.pallas import tpu as pltpu
from jax.sharding import PartitionSpec as P

loss_scale = 64.0
far = 136
near = 8
reach = 128
span = 296
window = 216
step = 80
keep = 88
lead = window - keep
freqs = 112
bins = 2 * freqs
columns = 1024
per_group = 16
parts = 16
lanes = 128
sub = 128
vmem_limit = 34 * 1024 * 1024


def split_np(table):
    upper = table.astype(ml_dtypes.bfloat16)
    lower = (table - upper.astype(np.float64)).astype(ml_dtypes.bfloat16)
    return upper, lower


def dft_tables():
    omega = 2.0 * np.pi * (np.arange(freqs) + 0.5) / bins
    rows = np.arange(window)
    angles = omega[:, None] * rows
    forward = np.concatenate([np.cos(angles), -np.sin(angles)])
    return forward, forward.T / freqs


def split_bf16(value):
    upper = value.astype(jnp.bfloat16)
    return upper, (value - upper.astype(jnp.float32)).astype(jnp.bfloat16)


def dot(left, right):
    return jnp.dot(left, right, preferred_element_type=jnp.float32)


def dot_t(left, right):
    return lax.dot_general(
        left, right, (((1,), (1,)), ((), ())), preferred_element_type=jnp.float32
    )


def dot_ta(left, right):
    return lax.dot_general(
        left, right, (((0,), (0,)), ((), ())), preferred_element_type=jnp.float32
    )


def taps(pieces, weight, member, start, count, sign):
    rows = jnp.concatenate([piece.astype(jnp.float32) for piece in pieces], axis=0)
    total = rows.shape[0]
    tap = [weight[offset, member : member + 1, :] for offset in range(7)]

    def moved(value, by):
        return pltpu.roll(value, (sign * by) % total, 0)

    one = moved(rows, 1)
    two = moved(rows, 2)
    tail = tap[4] * rows + tap[5] * one + tap[6] * two
    tail = tap[2] * rows + tap[3] * one + moved(tail, 2)
    tail = tap[0] * rows + tap[1] * one + moved(tail, 2)
    return tail[start : start + count]


def gains(med, analysis, block):
    groups = med.shape[1]
    channel = lax.broadcasted_iota(jnp.int32, (groups, columns), 1) + block * columns
    group = lax.broadcasted_iota(jnp.int32, (groups, columns), 0)
    expand = jnp.where(channel // per_group == group, 1.0, 0.0).astype(jnp.bfloat16)
    wide = dot(med, expand).astype(jnp.bfloat16)
    count = med.shape[0]
    both = dot(analysis[:, :count], wide)
    return both[:bins] + both[bins:]


def in_hbm(array):
    return pltpu.with_memory_space_constraint(array, pltpu.HBM)


def thirds(value):
    first, rest = split_bf16(value)
    second = (value - first.astype(jnp.float32)).astype(jnp.bfloat16)
    third = (value - first.astype(jnp.float32) - second.astype(jnp.float32)).astype(jnp.bfloat16)
    pieces = [piece.astype(jnp.float32) for piece in (first, second, third)]
    blank = jnp.zeros((parts - 12, value.shape[1]), jnp.float32)
    return jnp.concatenate(pieces + [blank], axis=0).astype(jnp.bfloat16)


def shard_kernel(out_weight, head, shard_out, head_out):
    coded = thirds(head[...])
    head_out[...] = coded
    found = dot_t(coded, out_weight[...])
    shard = thirds(found[0:4] + found[4:8] + found[8:12])
    for device in range(shard_out.shape[0]):
        shard_out[device] = shard


def local_kernel(
    length, q_edge, k, v, weight, key_out, value_out, products_out, to_right, to_left
):
    side = pl.program_id(1)

    def one(forward):
        sign = 1 if forward else -1
        for at in range(0, columns, sub):
            cols = slice(at, at + sub)
            taken = weight[:, :, cols]
            key_feat = taps((k[:, cols],), taken, 1, 0, length, sign)
            value_feat = taps((v[:, cols],), taken, 2, 0, length, sign)
            key_out[:, cols] = key_feat.astype(jnp.bfloat16)
            value_out[:, cols] = value_feat.astype(jnp.bfloat16)
            products_out[:, cols] = (key_feat * value_feat).astype(jnp.bfloat16)
        main, other = (to_right, to_left) if forward else (to_left, to_right)
        main_at = length - near if forward else 0
        other_at = 0 if forward else length - near
        first = length - reach if forward else 0
        main[0:reach, :] = products_out[first : first + reach, :]
        main[reach : reach + near, :] = q_edge[...]
        main[reach + near : reach + 2 * near, :] = k[main_at : main_at + near, :]
        main[reach + 2 * near : reach + 3 * near, :] = v[main_at : main_at + near, :]
        other[reach + 3 * near : reach + 4 * near, :] = k[other_at : other_at + near, :]
        other[reach + 4 * near : reach + 5 * near, :] = v[other_at : other_at + near, :]

    pl.when(side == 0)(functools.partial(one, True))
    pl.when(side == 1)(functools.partial(one, False))


def gate_kernel(length, q, s, weight, head_rows, gate_out, sums_out):
    block = pl.program_id(0)
    side = pl.program_id(1)

    def one(forward):
        for at in range(0, columns, sub):
            cols = slice(at, at + sub)
            gate = taps((q[:, cols],), weight[:, :, cols], 0, 0, length, 1 if forward else -1)
            gate_out[:, cols] = gate.astype(jnp.bfloat16)
        side_at = 0 if forward else 1
        term = dot_t(s[...], head_rows[...])

        @pl.when(block == 0)
        def _():
            sums_out[side_at] = term

        @pl.when(block > 0)
        def _():
            sums_out[side_at] += term

    pl.when(side == 0)(functools.partial(one, True))
    pl.when(side == 1)(functools.partial(one, False))


def class_block(class_rows):
    return jnp.concatenate([class_rows[piece] for piece in range(class_rows.shape[0])], axis=1)


def long_conv(rows_ref, spectrum, analysis, synthesis, causal):
    gain_re = spectrum[0:freqs, :]
    gain_im = spectrum[freqs:bins, :]
    if not causal:
        gain_im = -gain_im
    pieces = []
    for index in range(2):
        both = dot(analysis[...], rows_ref[index * step : index * step + window, :])
        re = both[:freqs] + both[bins : bins + freqs]
        im = both[freqs:bins] + both[bins + freqs :]
        mixed = jnp.concatenate([re * gain_re - im * gain_im, re * gain_im + im * gain_re], axis=0)
        high, low = split_bf16(mixed)
        both = dot(synthesis[...], high)
        piece = both[:keep] + both[keep:] + dot(synthesis[:keep], low)
        pieces.append(piece[:step] if index == 0 else piece)
    return jnp.concatenate(pieces, axis=0)


def kept(flag, piece):
    return jnp.where(flag, piece, jnp.zeros_like(piece))


def forward_kernel(
    length, inner, q_edge, k_low, k_high, v_low, v_high, local, first_gate, left, right, weight,
    class_rows, stream_sums, med, target, analysis, synth_c, synth_a, fold,
    gate_out, gated_out, mix_out, key_rim, value_rim, grad_out,
    products, spectrum, sums,
):
    block = pl.program_id(0)
    side = pl.program_id(1)

    @pl.when((block == 0) & (side == 0))
    def _():
        sums[...] = stream_sums[...]

    @pl.when(side == 0)
    def _():
        spectrum[...] = gains(med[...], analysis, block)

    def one(forward):
        main, other = (left, right) if forward else (right, left)
        left_flag, right_flag = inner[0] > 0, inner[1] > 0
        main_flag, other_flag = (left_flag, right_flag) if forward else (right_flag, left_flag)
        sign = 1 if forward else -1
        wide = jnp.float32

        def edges(low, high, member):
            at = reach + member * near
            beside_main = kept(main_flag, main[at : at + near, :].astype(wide))
            at = reach + (2 + member) * near
            beside_other = kept(other_flag, other[at : at + near, :].astype(wide))
            before, after = (
                (beside_main, beside_other) if forward else (beside_other, beside_main)
            )
            found = taps(
                (before, low[...], high[...], after), weight, member, 0, 4 * near, sign
            )
            if forward:
                return found[near : 2 * near], found[3 * near :]
            return found[2 * near : 3 * near], found[:near]

        key_fix, key_beyond = edges(k_low, k_high, 1)
        value_fix, value_beyond = edges(v_low, v_high, 2)
        key_rim[0:near, :] = key_fix.astype(jnp.bfloat16)
        key_rim[near:, :] = key_beyond.astype(jnp.bfloat16)
        value_rim[0:near, :] = value_fix.astype(jnp.bfloat16)
        value_rim[near:, :] = value_beyond.astype(jnp.bfloat16)
        halo = kept(main_flag, main[0:reach, :].astype(wide)).astype(jnp.bfloat16)
        fixed = (key_fix * value_fix).astype(jnp.bfloat16)
        beyond = (key_beyond * value_beyond).astype(jnp.bfloat16)
        q_near = kept(main_flag, main[reach : reach + near, :].astype(wide))
        if forward:
            products[0:reach, :] = halo
            products[reach : reach + near, :] = fixed
            products[reach + near : reach + length, :] = local[near:, :]
            products[reach + length :, :] = beyond
            gate = taps((q_near, q_edge[...]), weight, 0, near, near, sign)
            gate_out[0:near, :] = gate.astype(jnp.bfloat16)
            gate_out[near:, :] = first_gate[near:, :]
        else:
            products[0:near, :] = beyond
            products[near:length, :] = local[: length - near, :]
            products[length : length + near, :] = fixed
            products[length + near :, :] = halo
            gate = taps((q_edge[...], q_near), weight, 0, 0, near, sign)
            gate_out[0 : length - near, :] = first_gate[: length - near, :]
            gate_out[length - near :, :] = gate.astype(jnp.bfloat16)
        mix = long_conv(products, spectrum, analysis, synth_c if forward else synth_a, forward)
        mix = mix[:length] if forward else mix[near:]
        mix_out[...] = mix.astype(jnp.bfloat16)
        gated = (gate_out[...].astype(jnp.float32) * mix).astype(jnp.bfloat16)
        gated_out[...] = gated
        sums[0 if forward else 1] += dot_t(gated, class_block(class_rows))

    pl.when(side == 0)(functools.partial(one, True))
    pl.when(side == 1)(functools.partial(one, False))

    @pl.when((block == pl.num_programs(0) - 1) & (side == 1))
    def _():
        exact = lax.Precision.HIGHEST
        logits = jnp.dot(
            sums[0], fold[0], precision=exact, preferred_element_type=jnp.float32
        ) + jnp.dot(sums[1], fold[1], precision=exact, preferred_element_type=jnp.float32)
        logits = jnp.transpose(logits)[:8]
        row = lax.broadcasted_iota(jnp.int32, logits.shape, 0)
        valid = row < 4
        top = jnp.max(jnp.where(valid, logits, -jnp.inf), axis=0, keepdims=True)
        exponent = jnp.where(valid, jnp.exp(logits - top), 0.0)
        softmax_out = exponent / jnp.sum(exponent, axis=0, keepdims=True)
        one_hot = jnp.where(row == target[...], 1.0, 0.0)
        grad_out[...] = loss_scale * (softmax_out - one_hot)


def middle_kernel(
    length, gate, gated, mix, class_rows, grad, place,
    partial_out, mix_grad_out, gate_grad_out, to_left, to_right,
    turned, coded,
):
    block = pl.program_id(0)
    side = pl.program_id(1)

    @pl.when((block == 0) & (side == 0))
    def _():
        high, low = split_bf16(grad[...])
        for side_at in range(2):
            coded[side_at] = (
                dot_ta(high, place[side_at, 0]) + dot_ta(low, place[side_at, 1])
            ).astype(jnp.bfloat16)
        turned[0] = grad[...]
        for lane in range(4):
            turned[1, lane : lane + 1, :] = grad[3 - lane : 4 - lane, :]
        turned[1, 4:8, :] = jnp.zeros((4, length), jnp.float32)

    def one(forward):
        high, low = split_bf16(turned[0 if forward else 1])
        term = dot(high, gated[...]) + dot(low, gated[...])
        for piece in range(columns // lanes):
            cut = term[:, piece * lanes : piece * lanes + lanes]
            if forward:
                partial_out[piece] = cut
            else:
                partial_out[piece] += cut
        classes = class_block(class_rows)
        grads = dot(coded[0 if forward else 1], jnp.concatenate([classes, classes], axis=0))
        mix_grad = (grads * gate[...].astype(jnp.float32)).astype(jnp.bfloat16)
        gate_grad = (grads * mix[...].astype(jnp.float32)).astype(jnp.bfloat16)
        mix_grad_out[...] = mix_grad
        gate_grad_out[...] = gate_grad
        if forward:
            to_left[0:far, :] = mix_grad[:far]
            to_left[far:, :] = gate_grad[:near]
        else:
            to_right[0:far, :] = mix_grad[length - far :]
            to_right[far:, :] = gate_grad[length - near :]

    pl.when(side == 0)(functools.partial(one, True))
    pl.when(side == 1)(functools.partial(one, False))


def backward_kernel(
    length, forward, inner, mix_grad, gate_grad, halo, key_feat, value_feat, key_rim, value_rim,
    weight, med, analysis, synthesis, *rest,
):
    query_out, key_out, value_out, extended, spectrum = rest[-5:]
    spectrum[...] = gains(med[...], analysis, pl.program_id(0))
    flag = (inner[1] if forward else inner[0]) > 0
    start = 0 if forward else near
    sign = -1 if forward else 1
    far_rows = kept(flag, halo[0:far, :].astype(jnp.float32)).astype(jnp.bfloat16)
    if forward:
        extended[0:length, :] = mix_grad[...]
        extended[length:, :] = far_rows
    else:
        extended[0:far, :] = far_rows
        extended[far:, :] = mix_grad[...]
    for at in range(0, columns, sub):
        cols = slice(at, at + sub)
        rim = kept(flag, halo[far:, cols].astype(jnp.float32))
        pieces = (gate_grad[:, cols], rim) if forward else (rim, gate_grad[:, cols])
        query_out[:, cols] = taps(pieces, weight[:, :, cols], 0, start, length, sign).astype(
            jnp.bfloat16
        )
    back = long_conv(extended, spectrum, analysis, synthesis, not forward)
    for at in range(0, columns, sub):
        cols = slice(at, at + sub)
        for member, feat, edge, out in (
            (1, value_feat, value_rim, key_out),
            (2, key_feat, key_rim, value_out),
        ):
            fix, beyond = edge[0:near, cols], edge[near:, cols]
            if forward:
                pieces = (fix, feat[near:, cols], beyond)
            else:
                pieces = (beyond, feat[: length - near, cols], fix)
            joined = jnp.concatenate([piece.astype(jnp.float32) for piece in pieces], axis=0)
            out[:, cols] = taps(
                (back[:, cols] * joined,), weight[:, :, cols], member, start, length, sign
            ).astype(jnp.bfloat16)


def final_kernel(terms, head, out):
    total = jnp.sum(terms[...], axis=0)
    out[...] = lax.dot_general(
        total[:4],
        head[...] * (1.0 / loss_scale),
        (((0,), (0,)), ((), ())),
        precision=lax.Precision.HIGHEST,
        preferred_element_type=jnp.float32,
    )


def per_device(query, key, value, stream, targets, short_filter, med_filter, out_weight, head):
    length = query.shape[1]
    channels = query.shape[2]
    half = channels // 2
    blocks = half // columns
    count = lax.axis_size("seq")
    owners = lax.axis_size("fsdp")
    own = half // owners
    rightward = [(i, (i + 1) % count) for i in range(count)]
    leftward = [((i + 1) % count, i) for i in range(count)]
    query, key, value, stream = query[0], key[0], value[0], stream[0]
    bf16, f32 = jnp.bfloat16, jnp.float32
    packed = reach + 5 * near
    shape = jax.ShapeDtypeStruct
    whole = pl.BlockSpec(memory_space=pltpu.VMEM)
    scalars = pl.BlockSpec(memory_space=pltpu.SMEM)
    untouched = pl.BlockSpec(memory_space=pl.ANY)
    query, key, value, stream = in_hbm(query), in_hbm(key), in_hbm(value), in_hbm(stream)
    limit = pltpu.CompilerParams(vmem_limit_bytes=vmem_limit)
    params = pltpu.CompilerParams(
        dimension_semantics=("arbitrary", "arbitrary"), vmem_limit_bytes=vmem_limit
    )

    def full(array):
        rank = len(array.shape)
        return pl.BlockSpec(array.shape, lambda *_: (0,) * rank)

    def by_channel(rows):
        return pl.BlockSpec((rows, columns), lambda b, s: (0, s * blocks + b))

    def edge_rows(first, last):
        return pl.BlockSpec(
            (near, columns), lambda b, s: (first + (last - first) * s, s * blocks + b)
        )

    def by_half(rows):
        return pl.BlockSpec((rows, columns), lambda b, s: (0, b))

    def by_owner(rows):
        return pl.BlockSpec((columns // lanes, rows, lanes), lambda b, s: (b, 0, 0))

    weight_spec = pl.BlockSpec(short_filter.shape[:2] + (columns,), lambda b, s: (0, 0, b))
    end = length // near - 1
    local_rows = shape((length, channels), bf16)

    key_feat, value_feat, products, to_right, to_left = pl.pallas_call(
        functools.partial(local_kernel, length),
        grid=(blocks, 2),
        in_specs=[edge_rows(end, 0), by_channel(length), by_channel(length), weight_spec],
        out_specs=[by_channel(length)] * 3 + [by_half(packed)] * 2,
        out_shape=[local_rows] * 3 + [shape((packed, half), bf16)] * 2,
        compiler_params=params,
        name="local_features",
    )(query, key, value, short_filter)

    from_left = lax.ppermute(to_right, "seq", rightward)
    from_right = lax.ppermute(to_left, "seq", leftward)

    shard, head_rows = pl.pallas_call(
        shard_kernel,
        in_specs=[whole] * 2,
        out_specs=[whole] * 2,
        out_shape=[shape((owners, parts, own), bf16), shape((parts, half), bf16)],
        compiler_params=limit,
        name="shard",
    )(out_weight, head)
    class_rows = lax.all_to_all(shard, "fsdp", 0, 0, tiled=True)
    if own != lanes:
        class_rows = class_rows.reshape(owners, parts, -1, lanes).transpose(0, 2, 1, 3)
        class_rows = class_rows.reshape(-1, parts, lanes)

    sums_shape = shape((2, length, parts), f32)
    first_gate, stream_sums = pl.pallas_call(
        functools.partial(gate_kernel, length),
        grid=(blocks, 2),
        in_specs=[by_channel(length)] * 2 + [weight_spec, by_half(parts)],
        out_specs=[by_channel(length), full(sums_shape)],
        out_shape=[local_rows, sums_shape],
        compiler_params=params,
        name="gate_and_stream_logits",
    )(query, stream, short_filter, head_rows)

    position = lax.axis_index("seq")
    inner = jnp.stack([position > 0, position < count - 1]).astype(jnp.int32)

    forward, inverse = dft_tables()
    analysis = jnp.asarray(np.concatenate(split_np(forward)))
    synth_c = jnp.asarray(np.concatenate(split_np(inverse[lead:])))
    synth_a = jnp.asarray(np.concatenate(split_np(inverse[:keep])))

    fold = np.zeros((2, parts, 128), np.float32)
    place = np.zeros((2, 2, 8, 2 * parts), np.float32)
    for lane in range(4):
        for part in range(3):
            fold[0, 4 * part + lane, lane] = 1.0
            fold[1, 4 * part + 3 - lane, lane] = 1.0
            for level in range(2):
                place[0, level, lane, level * parts + 4 * part + lane] = 1.0
                place[1, level, 3 - lane, level * parts + 4 * part + lane] = 1.0
    place = jnp.asarray(place.astype(ml_dtypes.bfloat16))

    grad_shape = shape((8, length), f32)
    gate, gated, mix, key_rim, value_rim, grad = pl.pallas_call(
        functools.partial(forward_kernel, length),
        grid=(blocks, 2),
        in_specs=[scalars, edge_rows(0, end)]
        + [edge_rows(0, 0), edge_rows(end, end)] * 2
        + [by_channel(length)] * 2
        + [by_half(packed)] * 2
        + [
            weight_spec, by_owner(parts), full(sums_shape), full(med_filter), full(targets),
            full(analysis), full(synth_c), full(synth_a), full(fold),
        ],
        out_specs=[by_channel(length)] * 3 + [by_channel(2 * near)] * 2 + [full(grad_shape)],
        out_shape=[local_rows] * 3 + [shape((2 * near, channels), bf16)] * 2 + [grad_shape],
        scratch_shapes=[
            pltpu.VMEM((span, columns), bf16),
            pltpu.VMEM((bins, columns), f32),
            pltpu.VMEM((2, length, parts), f32),
        ],
        compiler_params=params,
        name="mix_and_logits",
    )(
        inner, query, key, key, value, value, products, first_gate, from_left, from_right,
        short_filter, class_rows, stream_sums, med_filter, targets, analysis, synth_c, synth_a,
        jnp.asarray(fold),
    )

    partial, mix_grad, gate_grad, to_left, to_right = pl.pallas_call(
        functools.partial(middle_kernel, length),
        grid=(blocks, 2),
        in_specs=[by_channel(length)] * 3 + [by_owner(parts), full(grad), full(place)],
        out_specs=[by_owner(8)] + [by_channel(length)] * 2 + [by_half(far + near)] * 2,
        out_shape=[shape((half // lanes, 8, lanes), f32)]
        + [shape((length, channels), bf16)] * 2
        + [shape((far + near, half), bf16)] * 2,
        scratch_shapes=[
            pltpu.VMEM((2, 8, length), f32),
            pltpu.VMEM((2, length, 2 * parts), bf16),
        ],
        compiler_params=params,
        name="weight_partial_and_mix_grad",
    )(gate, gated, mix, class_rows, grad, place)

    grad_left = lax.ppermute(to_right, "seq", rightward)
    grad_right = lax.ppermute(to_left, "seq", leftward)
    if own != lanes:
        partial = partial.reshape(owners, -1, 8, lanes).transpose(0, 2, 1, 3)
        partial = partial.reshape(owners, 8, own)
    by_genome = lax.all_to_all(partial, "fsdp", 0, 0, tiled=True)

    def gradients(forward, mix_grad, halo, synthesis, earlier):
        base = 0 if forward else blocks

        def by_channel(rows):
            return pl.BlockSpec((rows, columns), lambda b: (0, base + b))

        in_specs = (
            [scalars]
            + [by_channel(length)] * 2
            + [pl.BlockSpec((far + near, columns), lambda b: (0, b))]
            + [by_channel(length)] * 2
            + [by_channel(2 * near)] * 2
            + [
                pl.BlockSpec(short_filter.shape[:2] + (columns,), lambda b: (0, 0, b)),
                full(med_filter), full(analysis), full(synthesis),
            ]
            + [untouched] * len(earlier)
        )
        taken = len(in_specs) - len(earlier)
        return pl.pallas_call(
            functools.partial(backward_kernel, length, forward),
            grid=(blocks,),
            in_specs=in_specs,
            out_specs=[by_channel(length)] * 3,
            out_shape=[local_rows] * 3,
            scratch_shapes=[pltpu.VMEM((span, columns), bf16), pltpu.VMEM((bins, columns), f32)],
            input_output_aliases={taken + at: at for at in range(len(earlier))},
            compiler_params=pltpu.CompilerParams(
                dimension_semantics=("arbitrary",), vmem_limit_bytes=vmem_limit
            ),
            name="gradients_forward" if forward else "gradients_reverse",
        )(
            inner, in_hbm(mix_grad), in_hbm(gate_grad), halo, in_hbm(key_feat),
            in_hbm(value_feat), key_rim, value_rim, short_filter, med_filter, analysis,
            synthesis, *earlier,
        )

    grads = gradients(True, mix_grad, grad_right, synth_a, ())
    by_genome, grads = lax.optimization_barrier((by_genome, tuple(grads)))
    over_genomes = jnp.sum(by_genome, axis=0)
    spread = jnp.broadcast_to(over_genomes, (count,) + over_genomes.shape)
    spread, mix_grad = lax.optimization_barrier((spread, mix_grad))
    terms = lax.all_to_all(spread, "seq", 0, 0, tiled=True)
    grads = gradients(False, mix_grad, grad_left, synth_c, grads)
    terms, grads = lax.optimization_barrier((terms, tuple(grads)))
    query_grad, key_grad, value_grad = grads
    out_grad = pl.pallas_call(
        final_kernel,
        in_specs=[whole] * 2,
        out_specs=whole,
        out_shape=shape((own, half), f32),
        compiler_params=limit,
        name="final",
    )(terms, head)
    return query_grad[None], key_grad[None], value_grad[None], out_grad


def solution(mesh):
    rows = P("fsdp", "seq", None)
    placed = (rows, rows, rows, rows, P("fsdp", "seq"), P(), P(), P("fsdp", None), P())
    return jax.shard_map(
        per_device,
        mesh=mesh,
        in_specs=placed,
        out_specs=(rows, rows, rows, P("fsdp", None)),
        check_vma=False,
    )
```

```python
import functools

import jax
import jax.numpy as jnp
import ml_dtypes
import numpy as np
from jax import lax
from jax.experimental import pallas as pl
from jax.experimental.pallas import tpu as pltpu
from jax.sharding import PartitionSpec as P

loss_scale = 64.0
far = 136
near = 8
reach = 128
span = 296
window = 216
step = 80
keep = 88
lead = window - keep
freqs = 112
bins = 2 * freqs
columns = 1024
per_group = 16
parts = 16
lanes = 128
sub = 128
vmem_limit = 34 * 1024 * 1024


def split_np(table):
    upper = table.astype(ml_dtypes.bfloat16)
    lower = (table - upper.astype(np.float64)).astype(ml_dtypes.bfloat16)
    return upper, lower


def dft_tables():
    omega = 2.0 * np.pi * (np.arange(freqs) + 0.5) / bins
    rows = np.arange(window)
    angles = omega[:, None] * rows
    forward = np.concatenate([np.cos(angles), -np.sin(angles)])
    return forward, forward.T / freqs


def split_bf16(value):
    upper = value.astype(jnp.bfloat16)
    return upper, (value - upper.astype(jnp.float32)).astype(jnp.bfloat16)


def dot(left, right):
    return jnp.dot(left, right, preferred_element_type=jnp.float32)


def dot_t(left, right):
    return lax.dot_general(
        left, right, (((1,), (1,)), ((), ())), preferred_element_type=jnp.float32
    )


def dot_ta(left, right):
    return lax.dot_general(
        left, right, (((0,), (0,)), ((), ())), preferred_element_type=jnp.float32
    )


def taps(pieces, weight, member, start, count, sign):
    rows = jnp.concatenate([piece.astype(jnp.float32) for piece in pieces], axis=0)
    total = rows.shape[0]
    tap = [weight[member, offset : offset + 1, :] for offset in range(7)]

    def moved(value, by):
        return pltpu.roll(value, (sign * by) % total, 0)

    one = moved(rows, 1)
    two = moved(rows, 2)
    tail = tap[4] * rows + tap[5] * one + tap[6] * two
    tail = tap[2] * rows + tap[3] * one + moved(tail, 2)
    tail = tap[0] * rows + tap[1] * one + moved(tail, 2)
    return tail[start : start + count]


def gains(med, analysis, block):
    groups = med.shape[1]
    channel = lax.broadcasted_iota(jnp.int32, (groups, columns), 1) + block * columns
    group = lax.broadcasted_iota(jnp.int32, (groups, columns), 0)
    expand = jnp.where(channel // per_group == group, 1.0, 0.0).astype(jnp.bfloat16)
    wide = dot(med, expand).astype(jnp.bfloat16)
    count = med.shape[0]
    both = dot(analysis[:, :count], wide)
    return both[:bins] + both[bins:]


def in_hbm(array):
    return pltpu.with_memory_space_constraint(array, pltpu.HBM)


def thirds(value):
    first, rest = split_bf16(value)
    second = (value - first.astype(jnp.float32)).astype(jnp.bfloat16)
    third = (value - first.astype(jnp.float32) - second.astype(jnp.float32)).astype(jnp.bfloat16)
    pieces = [piece.astype(jnp.float32) for piece in (first, second, third)]
    blank = jnp.zeros((parts - 12, value.shape[1]), jnp.float32)
    return jnp.concatenate(pieces + [blank], axis=0).astype(jnp.bfloat16)


def shard_kernel(out_weight, head, shard_out, head_out):
    coded = thirds(head[...])
    head_out[...] = coded
    found = dot_t(coded, out_weight[...])
    shard = thirds(found[0:4] + found[4:8] + found[8:12])
    for device in range(shard_out.shape[0]):
        shard_out[device] = shard


def local_kernel(
    length, q_edge, k, v, weight, key_out, value_out, products_out, to_right, to_left
):
    side = pl.program_id(1)

    def one(forward):
        sign = 1 if forward else -1
        for at in range(0, columns, sub):
            cols = slice(at, at + sub)
            taken = weight[:, :, cols]
            key_feat = taps((k[:, cols],), taken, 1, 0, length, sign)
            value_feat = taps((v[:, cols],), taken, 2, 0, length, sign)
            key_out[:, cols] = key_feat.astype(jnp.bfloat16)
            value_out[:, cols] = value_feat.astype(jnp.bfloat16)
            products_out[:, cols] = (key_feat * value_feat).astype(jnp.bfloat16)
        main, other = (to_right, to_left) if forward else (to_left, to_right)
        main_at = length - near if forward else 0
        other_at = 0 if forward else length - near
        first = length - reach if forward else 0
        main[0:reach, :] = products_out[first : first + reach, :]
        main[reach : reach + near, :] = q_edge[...]
        main[reach + near : reach + 2 * near, :] = k[main_at : main_at + near, :]
        main[reach + 2 * near : reach + 3 * near, :] = v[main_at : main_at + near, :]
        other[reach + 3 * near : reach + 4 * near, :] = k[other_at : other_at + near, :]
        other[reach + 4 * near : reach + 5 * near, :] = v[other_at : other_at + near, :]

    pl.when(side == 0)(functools.partial(one, True))
    pl.when(side == 1)(functools.partial(one, False))


def gate_kernel(length, q, s, weight, head_rows, gate_out, sums_out):
    block = pl.program_id(0)
    side = pl.program_id(1)

    def one(forward):
        for at in range(0, columns, sub):
            cols = slice(at, at + sub)
            gate = taps((q[:, cols],), weight[:, :, cols], 0, 0, length, 1 if forward else -1)
            gate_out[:, cols] = gate.astype(jnp.bfloat16)
        side_at = 0 if forward else 1
        term = dot_t(s[...], head_rows[...])

        @pl.when(block == 0)
        def _():
            sums_out[side_at] = term

        @pl.when(block > 0)
        def _():
            sums_out[side_at] += term

    pl.when(side == 0)(functools.partial(one, True))
    pl.when(side == 1)(functools.partial(one, False))


def class_block(class_rows):
    return jnp.concatenate([class_rows[piece] for piece in range(class_rows.shape[0])], axis=1)


def long_conv(rows_ref, spectrum, analysis, synthesis, causal):
    gain_re = spectrum[0:freqs, :]
    gain_im = spectrum[freqs:bins, :]
    if not causal:
        gain_im = -gain_im
    pieces = []
    for index in range(2):
        both = dot(analysis[...], rows_ref[index * step : index * step + window, :])
        re = both[:freqs] + both[bins : bins + freqs]
        im = both[freqs:bins] + both[bins + freqs :]
        mixed = jnp.concatenate([re * gain_re - im * gain_im, re * gain_im + im * gain_re], axis=0)
        high, low = split_bf16(mixed)
        both = dot(synthesis[...], high)
        piece = both[:keep] + both[keep:] + dot(synthesis[:keep], low)
        pieces.append(piece[:step] if index == 0 else piece)
    return jnp.concatenate(pieces, axis=0)


def kept(flag, piece):
    return jnp.where(flag, piece, jnp.zeros_like(piece))


def forward_kernel(
    length, inner, q_edge, k_low, k_high, v_low, v_high, local, first_gate, left, right, weight,
    class_rows, stream_sums, med, target, analysis, synth_c, synth_a, fold,
    gate_out, gated_out, mix_out, key_rim, value_rim, grad_out,
    products, spectrum, sums,
):
    block = pl.program_id(0)
    side = pl.program_id(1)

    @pl.when((block == 0) & (side == 0))
    def _():
        sums[...] = stream_sums[...]

    @pl.when(side == 0)
    def _():
        spectrum[...] = gains(med[...], analysis, block)

    def one(forward):
        main, other = (left, right) if forward else (right, left)
        left_flag, right_flag = inner[0] > 0, inner[1] > 0
        main_flag, other_flag = (left_flag, right_flag) if forward else (right_flag, left_flag)
        sign = 1 if forward else -1
        wide = jnp.float32

        def edges(low, high, member):
            at = reach + member * near
            beside_main = kept(main_flag, main[at : at + near, :].astype(wide))
            at = reach + (2 + member) * near
            beside_other = kept(other_flag, other[at : at + near, :].astype(wide))
            before, after = (
                (beside_main, beside_other) if forward else (beside_other, beside_main)
            )
            found = taps(
                (before, low[...], high[...], after), weight, member, 0, 4 * near, sign
            )
            if forward:
                return found[near : 2 * near], found[3 * near :]
            return found[2 * near : 3 * near], found[:near]

        key_fix, key_beyond = edges(k_low, k_high, 1)
        value_fix, value_beyond = edges(v_low, v_high, 2)
        key_rim[0:near, :] = key_fix.astype(jnp.bfloat16)
        key_rim[near:, :] = key_beyond.astype(jnp.bfloat16)
        value_rim[0:near, :] = value_fix.astype(jnp.bfloat16)
        value_rim[near:, :] = value_beyond.astype(jnp.bfloat16)
        halo = kept(main_flag, main[0:reach, :].astype(wide)).astype(jnp.bfloat16)
        fixed = (key_fix * value_fix).astype(jnp.bfloat16)
        beyond = (key_beyond * value_beyond).astype(jnp.bfloat16)
        q_near = kept(main_flag, main[reach : reach + near, :].astype(wide))
        if forward:
            products[0:reach, :] = halo
            products[reach : reach + near, :] = fixed
            products[reach + near : reach + length, :] = local[near:, :]
            products[reach + length :, :] = beyond
            gate = taps((q_near, q_edge[...]), weight, 0, near, near, sign)
            gate_out[0:near, :] = gate.astype(jnp.bfloat16)
            gate_out[near:, :] = first_gate[near:, :]
        else:
            products[0:near, :] = beyond
            products[near:length, :] = local[: length - near, :]
            products[length : length + near, :] = fixed
            products[length + near :, :] = halo
            gate = taps((q_edge[...], q_near), weight, 0, 0, near, sign)
            gate_out[0 : length - near, :] = first_gate[: length - near, :]
            gate_out[length - near :, :] = gate.astype(jnp.bfloat16)
        mix = long_conv(products, spectrum, analysis, synth_c if forward else synth_a, forward)
        mix = mix[:length] if forward else mix[near:]
        mix_out[...] = mix.astype(jnp.bfloat16)
        gated = (gate_out[...].astype(jnp.float32) * mix).astype(jnp.bfloat16)
        gated_out[...] = gated
        sums[0 if forward else 1] += dot_t(gated, class_block(class_rows))

    pl.when(side == 0)(functools.partial(one, True))
    pl.when(side == 1)(functools.partial(one, False))

    @pl.when((block == pl.num_programs(0) - 1) & (side == 1))
    def _():
        exact = lax.Precision.HIGHEST
        logits = jnp.dot(
            sums[0], fold[0], precision=exact, preferred_element_type=jnp.float32
        ) + jnp.dot(sums[1], fold[1], precision=exact, preferred_element_type=jnp.float32)
        logits = jnp.transpose(logits)[:8]
        row = lax.broadcasted_iota(jnp.int32, logits.shape, 0)
        valid = row < 4
        top = jnp.max(jnp.where(valid, logits, -jnp.inf), axis=0, keepdims=True)
        exponent = jnp.where(valid, jnp.exp(logits - top), 0.0)
        softmax_out = exponent / jnp.sum(exponent, axis=0, keepdims=True)
        one_hot = jnp.where(row == target[...], 1.0, 0.0)
        grad_out[...] = loss_scale * (softmax_out - one_hot)


def middle_kernel(
    length, gate, gated, mix, class_rows, grad, place,
    partial_out, mix_grad_out, gate_grad_out, to_left, to_right,
    turned, coded,
):
    block = pl.program_id(0)
    side = pl.program_id(1)

    @pl.when((block == 0) & (side == 0))
    def _():
        high, low = split_bf16(grad[...])
        for side_at in range(2):
            coded[side_at] = (
                dot_ta(high, place[side_at, 0]) + dot_ta(low, place[side_at, 1])
            ).astype(jnp.bfloat16)
        turned[0] = grad[...]
        for lane in range(4):
            turned[1, lane : lane + 1, :] = grad[3 - lane : 4 - lane, :]
        turned[1, 4:8, :] = jnp.zeros((4, length), jnp.float32)

    def one(forward):
        high, low = split_bf16(turned[0 if forward else 1])
        term = dot(high, gated[...]) + dot(low, gated[...])
        for piece in range(columns // lanes):
            cut = term[:, piece * lanes : piece * lanes + lanes]
            if forward:
                partial_out[piece] = cut
            else:
                partial_out[piece] += cut
        classes = class_block(class_rows)
        grads = dot(coded[0 if forward else 1], jnp.concatenate([classes, classes], axis=0))
        mix_grad = (grads * gate[...].astype(jnp.float32)).astype(jnp.bfloat16)
        gate_grad = (grads * mix[...].astype(jnp.float32)).astype(jnp.bfloat16)
        mix_grad_out[...] = mix_grad
        gate_grad_out[...] = gate_grad
        if forward:
            to_left[0:far, :] = mix_grad[:far]
            to_left[far:, :] = gate_grad[:near]
        else:
            to_right[0:far, :] = mix_grad[length - far :]
            to_right[far:, :] = gate_grad[length - near :]

    pl.when(side == 0)(functools.partial(one, True))
    pl.when(side == 1)(functools.partial(one, False))


def backward_kernel(
    length, forward, inner, mix_grad, gate_grad, halo, key_feat, value_feat, key_rim, value_rim,
    weight, med, analysis, synthesis, *rest,
):
    query_out, key_out, value_out, extended, spectrum = rest[-5:]
    spectrum[...] = gains(med[...], analysis, pl.program_id(0))
    flag = (inner[1] if forward else inner[0]) > 0
    start = 0 if forward else near
    sign = -1 if forward else 1
    far_rows = kept(flag, halo[0:far, :].astype(jnp.float32)).astype(jnp.bfloat16)
    if forward:
        extended[0:length, :] = mix_grad[...]
        extended[length:, :] = far_rows
    else:
        extended[0:far, :] = far_rows
        extended[far:, :] = mix_grad[...]
    for at in range(0, columns, sub):
        cols = slice(at, at + sub)
        rim = kept(flag, halo[far:, cols].astype(jnp.float32))
        pieces = (gate_grad[:, cols], rim) if forward else (rim, gate_grad[:, cols])
        query_out[:, cols] = taps(pieces, weight[:, :, cols], 0, start, length, sign).astype(
            jnp.bfloat16
        )
    back = long_conv(extended, spectrum, analysis, synthesis, not forward)
    for at in range(0, columns, sub):
        cols = slice(at, at + sub)
        for member, feat, edge, out in (
            (1, value_feat, value_rim, key_out),
            (2, key_feat, key_rim, value_out),
        ):
            fix, beyond = edge[0:near, cols], edge[near:, cols]
            if forward:
                pieces = (fix, feat[near:, cols], beyond)
            else:
                pieces = (beyond, feat[: length - near, cols], fix)
            joined = jnp.concatenate([piece.astype(jnp.float32) for piece in pieces], axis=0)
            out[:, cols] = taps(
                (back[:, cols] * joined,), weight[:, :, cols], member, start, length, sign
            ).astype(jnp.bfloat16)


def final_kernel(terms, head, out):
    total = jnp.sum(terms[...], axis=0)
    out[...] = lax.dot_general(
        total[:4],
        head[...] * (1.0 / loss_scale),
        (((0,), (0,)), ((), ())),
        precision=lax.Precision.HIGHEST,
        preferred_element_type=jnp.float32,
    )


def per_device(query, key, value, stream, targets, short_filter, med_filter, out_weight, head):
    length = query.shape[1]
    channels = query.shape[2]
    half = channels // 2
    blocks = half // columns
    count = lax.axis_size("seq")
    owners = lax.axis_size("fsdp")
    own = half // owners
    rightward = [(i, (i + 1) % count) for i in range(count)]
    leftward = [((i + 1) % count, i) for i in range(count)]
    query, key, value, stream = query[0], key[0], value[0], stream[0]
    short_filter = short_filter.transpose(1, 0, 2)
    bf16, f32 = jnp.bfloat16, jnp.float32
    packed = reach + 5 * near
    shape = jax.ShapeDtypeStruct
    whole = pl.BlockSpec(memory_space=pltpu.VMEM)
    scalars = pl.BlockSpec(memory_space=pltpu.SMEM)
    untouched = pl.BlockSpec(memory_space=pl.ANY)
    query, key, value = in_hbm(query), in_hbm(key), in_hbm(value)
    limit = pltpu.CompilerParams(vmem_limit_bytes=vmem_limit)
    params = pltpu.CompilerParams(
        dimension_semantics=("arbitrary", "arbitrary"), vmem_limit_bytes=vmem_limit
    )

    def full(array):
        rank = len(array.shape)
        return pl.BlockSpec(array.shape, lambda *_: (0,) * rank)

    def by_channel(rows):
        return pl.BlockSpec((rows, columns), lambda b, s: (0, s * blocks + b))

    def edge_rows(first, last):
        return pl.BlockSpec(
            (near, columns), lambda b, s: (first + (last - first) * s, s * blocks + b)
        )

    def by_half(rows):
        return pl.BlockSpec((rows, columns), lambda b, s: (0, b))

    def by_owner(rows):
        return pl.BlockSpec((columns // lanes, rows, lanes), lambda b, s: (b, 0, 0))

    weight_spec = pl.BlockSpec(short_filter.shape[:2] + (columns,), lambda b, s: (0, 0, b))
    end = length // near - 1
    local_rows = shape((length, channels), bf16)
    hbm_rows = pltpu.HBM((length, channels), bf16)

    shard, head_rows = pl.pallas_call(
        shard_kernel,
        in_specs=[whole] * 2,
        out_specs=[whole] * 2,
        out_shape=[shape((owners, parts, own), bf16), shape((parts, half), bf16)],
        compiler_params=limit,
        name="shard",
    )(out_weight, head)
    shard, key = lax.optimization_barrier((shard, key))
    class_rows = lax.all_to_all(shard, "fsdp", 0, 0, tiled=True)
    if own != lanes:
        class_rows = class_rows.reshape(owners, parts, -1, lanes).transpose(0, 2, 1, 3)
        class_rows = class_rows.reshape(-1, parts, lanes)

    key_feat, value_feat, products, to_right, to_left = pl.pallas_call(
        functools.partial(local_kernel, length),
        grid=(blocks, 2),
        in_specs=[edge_rows(end, 0), by_channel(length), by_channel(length), weight_spec],
        out_specs=[by_channel(length)] * 3 + [by_half(packed)] * 2,
        out_shape=[hbm_rows] * 2 + [local_rows] + [shape((packed, half), bf16)] * 2,
        compiler_params=params,
        name="local_features",
    )(query, key, value, short_filter)

    class_rows, to_right, to_left = lax.optimization_barrier((class_rows, to_right, to_left))
    from_left = lax.ppermute(to_right, "seq", rightward)
    from_right = lax.ppermute(to_left, "seq", leftward)

    sums_shape = shape((2, length, parts), f32)
    first_gate, stream_sums = pl.pallas_call(
        functools.partial(gate_kernel, length),
        grid=(blocks, 2),
        in_specs=[by_channel(length)] * 2 + [weight_spec, by_half(parts)],
        out_specs=[by_channel(length), full(sums_shape)],
        out_shape=[local_rows, sums_shape],
        compiler_params=params,
        name="gate_and_stream_logits",
    )(query, in_hbm(stream), short_filter, head_rows)

    position = lax.axis_index("seq")
    inner = jnp.stack([position > 0, position < count - 1]).astype(jnp.int32)

    forward, inverse = dft_tables()
    analysis = jnp.asarray(np.concatenate(split_np(forward)))
    synth_c = jnp.asarray(np.concatenate(split_np(inverse[lead:])))
    synth_a = jnp.asarray(np.concatenate(split_np(inverse[:keep])))

    fold = np.zeros((2, parts, 128), np.float32)
    place = np.zeros((2, 2, 8, 2 * parts), np.float32)
    for lane in range(4):
        for part in range(3):
            fold[0, 4 * part + lane, lane] = 1.0
            fold[1, 4 * part + 3 - lane, lane] = 1.0
            for level in range(2):
                place[0, level, lane, level * parts + 4 * part + lane] = 1.0
                place[1, level, 3 - lane, level * parts + 4 * part + lane] = 1.0
    place = jnp.asarray(place.astype(ml_dtypes.bfloat16))

    grad_shape = shape((8, length), f32)
    gate, gated, mix, key_rim, value_rim, grad = pl.pallas_call(
        functools.partial(forward_kernel, length),
        grid=(blocks, 2),
        in_specs=[scalars, edge_rows(0, end)]
        + [edge_rows(0, 0), edge_rows(end, end)] * 2
        + [by_channel(length)] * 2
        + [by_half(packed)] * 2
        + [
            weight_spec, by_owner(parts), full(sums_shape), full(med_filter), full(targets),
            full(analysis), full(synth_c), full(synth_a), full(fold),
        ],
        out_specs=[by_channel(length)] * 3 + [by_channel(2 * near)] * 2 + [full(grad_shape)],
        out_shape=[local_rows] * 3 + [shape((2 * near, channels), bf16)] * 2 + [grad_shape],
        scratch_shapes=[
            pltpu.VMEM((span, columns), bf16),
            pltpu.VMEM((bins, columns), f32),
            pltpu.VMEM((2, length, parts), f32),
        ],
        compiler_params=params,
        name="mix_and_logits",
    )(
        inner, query, key, key, value, value, products, first_gate, from_left, from_right,
        short_filter, class_rows, stream_sums, med_filter, targets, analysis, synth_c, synth_a,
        jnp.asarray(fold),
    )

    partial, mix_grad, gate_grad, to_left, to_right = pl.pallas_call(
        functools.partial(middle_kernel, length),
        grid=(blocks, 2),
        in_specs=[by_channel(length)] * 3 + [by_owner(parts), full(grad), full(place)],
        out_specs=[by_owner(8)] + [by_channel(length)] * 2 + [by_half(far + near)] * 2,
        out_shape=[shape((half // lanes, 8, lanes), f32)]
        + [hbm_rows] * 2
        + [shape((far + near, half), bf16)] * 2,
        scratch_shapes=[
            pltpu.VMEM((2, 8, length), f32),
            pltpu.VMEM((2, length, 2 * parts), bf16),
        ],
        compiler_params=params,
        name="weight_partial_and_mix_grad",
    )(gate, gated, mix, class_rows, grad, place)

    grad_left = lax.ppermute(to_right, "seq", rightward)
    grad_right = lax.ppermute(to_left, "seq", leftward)
    if own != lanes:
        partial = partial.reshape(owners, -1, 8, lanes).transpose(0, 2, 1, 3)
        partial = partial.reshape(owners, 8, own)
    by_genome = lax.all_to_all(partial, "fsdp", 0, 0, tiled=True)

    def gradients(forward, mix_grad, halo, synthesis, earlier):
        base = 0 if forward else blocks

        def by_channel(rows):
            return pl.BlockSpec((rows, columns), lambda b: (0, base + b))

        in_specs = (
            [scalars]
            + [by_channel(length)] * 2
            + [pl.BlockSpec((far + near, columns), lambda b: (0, b))]
            + [by_channel(length)] * 2
            + [by_channel(2 * near)] * 2
            + [
                pl.BlockSpec(short_filter.shape[:2] + (columns,), lambda b: (0, 0, b)),
                full(med_filter), full(analysis), full(synthesis),
            ]
            + [untouched] * len(earlier)
        )
        taken = len(in_specs) - len(earlier)
        return pl.pallas_call(
            functools.partial(backward_kernel, length, forward),
            grid=(blocks,),
            in_specs=in_specs,
            out_specs=[by_channel(length)] * 3,
            out_shape=[local_rows] * 3,
            scratch_shapes=[pltpu.VMEM((span, columns), bf16), pltpu.VMEM((bins, columns), f32)],
            input_output_aliases={taken + at: at for at in range(len(earlier))},
            compiler_params=pltpu.CompilerParams(
                dimension_semantics=("arbitrary",), vmem_limit_bytes=vmem_limit
            ),
            name="gradients_forward" if forward else "gradients_reverse",
        )(
            inner, in_hbm(mix_grad), in_hbm(gate_grad), halo, in_hbm(key_feat),
            in_hbm(value_feat), key_rim, value_rim, short_filter, med_filter, analysis,
            synthesis, *earlier,
        )

    grads = gradients(True, mix_grad, grad_right, synth_a, ())
    by_genome, grads = lax.optimization_barrier((by_genome, tuple(grads)))
    over_genomes = jnp.sum(by_genome, axis=0)
    spread = jnp.broadcast_to(over_genomes, (count,) + over_genomes.shape)
    spread, mix_grad = lax.optimization_barrier((spread, mix_grad))
    terms = lax.all_to_all(spread, "seq", 0, 0, tiled=True)
    grads = gradients(False, mix_grad, grad_left, synth_c, grads)
    terms, grads = lax.optimization_barrier((terms, tuple(grads)))
    query_grad, key_grad, value_grad = grads
    out_grad = pl.pallas_call(
        final_kernel,
        in_specs=[whole] * 2,
        out_specs=whole,
        out_shape=shape((own, half), f32),
        compiler_params=limit,
        name="final",
    )(terms, head)
    return query_grad[None], key_grad[None], value_grad[None], out_grad


def solution(mesh):
    rows = P("fsdp", "seq", None)
    placed = (rows, rows, rows, rows, P("fsdp", "seq"), P(), P(), P("fsdp", None), P())
    return jax.shard_map(
        per_device,
        mesh=mesh,
        in_specs=placed,
        out_specs=(rows, rows, rows, P("fsdp", None)),
        check_vma=False,
    )
```

```python
import functools

import jax
import jax.numpy as jnp
import ml_dtypes
import numpy as np
from jax import lax
from jax.experimental import pallas as pl
from jax.experimental.pallas import tpu as pltpu
from jax.sharding import PartitionSpec as P

loss_scale = 64.0
far = 136
near = 8
reach = 128
span = 296
window = 216
step = 80
keep = 88
lead = window - keep
freqs = 112
bins = 2 * freqs
columns = 1024
per_group = 16
parts = 16
lanes = 128
sub = 128
vmem_limit = 34 * 1024 * 1024


def split_np(table):
    upper = table.astype(ml_dtypes.bfloat16)
    lower = (table - upper.astype(np.float64)).astype(ml_dtypes.bfloat16)
    return upper, lower


def dft_tables():
    omega = 2.0 * np.pi * (np.arange(freqs) + 0.5) / bins
    rows = np.arange(window)
    angles = omega[:, None] * rows
    forward = np.concatenate([np.cos(angles), -np.sin(angles)])
    return forward, forward.T / freqs


def split_bf16(value):
    upper = value.astype(jnp.bfloat16)
    return upper, (value - upper.astype(jnp.float32)).astype(jnp.bfloat16)


def dot(left, right):
    return jnp.dot(left, right, preferred_element_type=jnp.float32)


def dot_t(left, right):
    return lax.dot_general(
        left, right, (((1,), (1,)), ((), ())), preferred_element_type=jnp.float32
    )


def dot_ta(left, right):
    return lax.dot_general(
        left, right, (((0,), (0,)), ((), ())), preferred_element_type=jnp.float32
    )


def taps(pieces, weight, member, start, count, sign):
    rows = jnp.concatenate([piece.astype(jnp.float32) for piece in pieces], axis=0)
    total = rows.shape[0]
    tap = [weight[member, offset : offset + 1, :] for offset in range(7)]

    def moved(value, by):
        return pltpu.roll(value, (sign * by) % total, 0)

    one = moved(rows, 1)
    two = moved(rows, 2)
    tail = tap[4] * rows + tap[5] * one + tap[6] * two
    tail = tap[2] * rows + tap[3] * one + moved(tail, 2)
    tail = tap[0] * rows + tap[1] * one + moved(tail, 2)
    return tail[start : start + count]


def gains(med, analysis, block):
    groups = med.shape[1]
    channel = lax.broadcasted_iota(jnp.int32, (groups, columns), 1) + block * columns
    group = lax.broadcasted_iota(jnp.int32, (groups, columns), 0)
    expand = jnp.where(channel // per_group == group, 1.0, 0.0).astype(jnp.bfloat16)
    wide = dot(med, expand).astype(jnp.bfloat16)
    count = med.shape[0]
    both = dot(analysis[:, :count], wide)
    return both[:bins] + both[bins:]


def in_hbm(array):
    return pltpu.with_memory_space_constraint(array, pltpu.HBM)


def thirds(value):
    first, rest = split_bf16(value)
    second = (value - first.astype(jnp.float32)).astype(jnp.bfloat16)
    third = (value - first.astype(jnp.float32) - second.astype(jnp.float32)).astype(jnp.bfloat16)
    pieces = [piece.astype(jnp.float32) for piece in (first, second, third)]
    blank = jnp.zeros((parts - 12, value.shape[1]), jnp.float32)
    return jnp.concatenate(pieces + [blank], axis=0).astype(jnp.bfloat16)


def shard_kernel(out_weight, head, shard_out, head_out):
    coded = thirds(head[...])
    head_out[...] = coded
    found = dot_t(coded, out_weight[...])
    shard = thirds(found[0:4] + found[4:8] + found[8:12])
    for device in range(shard_out.shape[0]):
        shard_out[device] = shard


def local_kernel(
    length, q_edge, k, v, weight, key_out, value_out, products_out, to_right, to_left
):
    side = pl.program_id(1)

    def one(forward):
        sign = 1 if forward else -1
        for at in range(0, columns, sub):
            cols = slice(at, at + sub)
            taken = weight[:, :, cols]
            key_feat = taps((k[:, cols],), taken, 1, 0, length, sign)
            value_feat = taps((v[:, cols],), taken, 2, 0, length, sign)
            key_out[:, cols] = key_feat.astype(jnp.bfloat16)
            value_out[:, cols] = value_feat.astype(jnp.bfloat16)
            products_out[:, cols] = (key_feat * value_feat).astype(jnp.bfloat16)
        main, other = (to_right, to_left) if forward else (to_left, to_right)
        main_at = length - near if forward else 0
        other_at = 0 if forward else length - near
        first = length - reach if forward else 0
        main[0:reach, :] = products_out[first : first + reach, :]
        main[reach : reach + near, :] = q_edge[...]
        main[reach + near : reach + 2 * near, :] = k[main_at : main_at + near, :]
        main[reach + 2 * near : reach + 3 * near, :] = v[main_at : main_at + near, :]
        other[reach + 3 * near : reach + 4 * near, :] = k[other_at : other_at + near, :]
        other[reach + 4 * near : reach + 5 * near, :] = v[other_at : other_at + near, :]

    pl.when(side == 0)(functools.partial(one, True))
    pl.when(side == 1)(functools.partial(one, False))


def gate_kernel(length, q, s, weight, head_rows, gate_out, sums_out):
    block = pl.program_id(0)
    side = pl.program_id(1)

    def one(forward):
        for at in range(0, columns, sub):
            cols = slice(at, at + sub)
            gate = taps((q[:, cols],), weight[:, :, cols], 0, 0, length, 1 if forward else -1)
            gate_out[:, cols] = gate.astype(jnp.bfloat16)
        side_at = 0 if forward else 1
        term = dot_t(s[...], head_rows[...])

        @pl.when(block == 0)
        def _():
            sums_out[side_at] = term

        @pl.when(block > 0)
        def _():
            sums_out[side_at] += term

    pl.when(side == 0)(functools.partial(one, True))
    pl.when(side == 1)(functools.partial(one, False))


def class_block(class_rows):
    return jnp.concatenate([class_rows[piece] for piece in range(class_rows.shape[0])], axis=1)


def long_conv(rows_ref, spectrum, analysis, synthesis, causal):
    gain_re = spectrum[0:freqs, :]
    gain_im = spectrum[freqs:bins, :]
    if not causal:
        gain_im = -gain_im
    pieces = []
    for index in range(2):
        both = dot(analysis[...], rows_ref[index * step : index * step + window, :])
        re = both[:freqs] + both[bins : bins + freqs]
        im = both[freqs:bins] + both[bins + freqs :]
        mixed = jnp.concatenate([re * gain_re - im * gain_im, re * gain_im + im * gain_re], axis=0)
        both = dot(synthesis[...], mixed.astype(jnp.bfloat16))
        piece = both[:keep] + both[keep:]
        pieces.append(piece[:step] if index == 0 else piece)
    return jnp.concatenate(pieces, axis=0)


def kept(flag, piece):
    return jnp.where(flag, piece, jnp.zeros_like(piece))


def forward_kernel(
    length, inner, q_edge, k_low, k_high, v_low, v_high, local, first_gate, left, right, weight,
    class_rows, stream_sums, med, target, analysis, synth_c, synth_a, fold,
    gate_out, gated_out, mix_out, key_rim, value_rim, grad_out,
    products, spectrum, sums,
):
    block = pl.program_id(0)
    side = pl.program_id(1)

    @pl.when((block == 0) & (side == 0))
    def _():
        sums[...] = stream_sums[...]

    @pl.when(side == 0)
    def _():
        spectrum[...] = gains(med[...], analysis, block)

    def one(forward):
        main, other = (left, right) if forward else (right, left)
        left_flag, right_flag = inner[0] > 0, inner[1] > 0
        main_flag, other_flag = (left_flag, right_flag) if forward else (right_flag, left_flag)
        sign = 1 if forward else -1
        wide = jnp.float32

        def edges(low, high, member):
            at = reach + member * near
            beside_main = kept(main_flag, main[at : at + near, :].astype(wide))
            at = reach + (2 + member) * near
            beside_other = kept(other_flag, other[at : at + near, :].astype(wide))
            before, after = (
                (beside_main, beside_other) if forward else (beside_other, beside_main)
            )
            found = taps(
                (before, low[...], high[...], after), weight, member, 0, 4 * near, sign
            )
            if forward:
                return found[near : 2 * near], found[3 * near :]
            return found[2 * near : 3 * near], found[:near]

        key_fix, key_beyond = edges(k_low, k_high, 1)
        value_fix, value_beyond = edges(v_low, v_high, 2)
        key_rim[0:near, :] = key_fix.astype(jnp.bfloat16)
        key_rim[near:, :] = key_beyond.astype(jnp.bfloat16)
        value_rim[0:near, :] = value_fix.astype(jnp.bfloat16)
        value_rim[near:, :] = value_beyond.astype(jnp.bfloat16)
        halo = kept(main_flag, main[0:reach, :].astype(wide)).astype(jnp.bfloat16)
        fixed = (key_fix * value_fix).astype(jnp.bfloat16)
        beyond = (key_beyond * value_beyond).astype(jnp.bfloat16)
        q_near = kept(main_flag, main[reach : reach + near, :].astype(wide))
        if forward:
            products[0:reach, :] = halo
            products[reach : reach + near, :] = fixed
            products[reach + near : reach + length, :] = local[near:, :]
            products[reach + length :, :] = beyond
            gate = taps((q_near, q_edge[...]), weight, 0, near, near, sign)
            gate_out[0:near, :] = gate.astype(jnp.bfloat16)
            gate_out[near:, :] = first_gate[near:, :]
        else:
            products[0:near, :] = beyond
            products[near:length, :] = local[: length - near, :]
            products[length : length + near, :] = fixed
            products[length + near :, :] = halo
            gate = taps((q_edge[...], q_near), weight, 0, 0, near, sign)
            gate_out[0 : length - near, :] = first_gate[: length - near, :]
            gate_out[length - near :, :] = gate.astype(jnp.bfloat16)
        mix = long_conv(products, spectrum, analysis, synth_c if forward else synth_a, forward)
        mix = mix[:length] if forward else mix[near:]
        mix_out[...] = mix.astype(jnp.bfloat16)
        gated = (gate_out[...].astype(jnp.float32) * mix).astype(jnp.bfloat16)
        gated_out[...] = gated
        sums[0 if forward else 1] += dot_t(gated, class_block(class_rows))

    pl.when(side == 0)(functools.partial(one, True))
    pl.when(side == 1)(functools.partial(one, False))

    @pl.when((block == pl.num_programs(0) - 1) & (side == 1))
    def _():
        exact = lax.Precision.HIGHEST
        logits = jnp.dot(
            sums[0], fold[0], precision=exact, preferred_element_type=jnp.float32
        ) + jnp.dot(sums[1], fold[1], precision=exact, preferred_element_type=jnp.float32)
        logits = jnp.transpose(logits)[:8]
        row = lax.broadcasted_iota(jnp.int32, logits.shape, 0)
        valid = row < 4
        top = jnp.max(jnp.where(valid, logits, -jnp.inf), axis=0, keepdims=True)
        exponent = jnp.where(valid, jnp.exp(logits - top), 0.0)
        softmax_out = exponent / jnp.sum(exponent, axis=0, keepdims=True)
        one_hot = jnp.where(row == target[...], 1.0, 0.0)
        grad_out[...] = loss_scale * (softmax_out - one_hot)


def middle_kernel(
    length, gate, gated, mix, class_rows, grad, place,
    partial_out, mix_grad_out, gate_grad_out, to_left, to_right,
    turned, coded,
):
    block = pl.program_id(0)
    side = pl.program_id(1)

    @pl.when((block == 0) & (side == 0))
    def _():
        high, low = split_bf16(grad[...])
        for side_at in range(2):
            coded[side_at] = (
                dot_ta(high, place[side_at, 0]) + dot_ta(low, place[side_at, 1])
            ).astype(jnp.bfloat16)
        turned[0] = grad[...]
        for lane in range(4):
            turned[1, lane : lane + 1, :] = grad[3 - lane : 4 - lane, :]
        turned[1, 4:8, :] = jnp.zeros((4, length), jnp.float32)

    def one(forward):
        high, low = split_bf16(turned[0 if forward else 1])
        term = dot(high, gated[...]) + dot(low, gated[...])
        for piece in range(columns // lanes):
            cut = term[:, piece * lanes : piece * lanes + lanes]
            if forward:
                partial_out[piece] = cut
            else:
                partial_out[piece] += cut
        classes = class_block(class_rows)
        grads = dot(coded[0 if forward else 1], jnp.concatenate([classes, classes], axis=0))
        mix_grad = (grads * gate[...].astype(jnp.float32)).astype(jnp.bfloat16)
        gate_grad = (grads * mix[...].astype(jnp.float32)).astype(jnp.bfloat16)
        mix_grad_out[...] = mix_grad
        gate_grad_out[...] = gate_grad
        if forward:
            to_left[0:far, :] = mix_grad[:far]
            to_left[far:, :] = gate_grad[:near]
        else:
            to_right[0:far, :] = mix_grad[length - far :]
            to_right[far:, :] = gate_grad[length - near :]

    pl.when(side == 0)(functools.partial(one, True))
    pl.when(side == 1)(functools.partial(one, False))


def backward_kernel(
    length, forward, inner, mix_grad, gate_grad, halo, key_feat, value_feat, key_rim, value_rim,
    weight, med, analysis, synthesis, *rest,
):
    query_out, key_out, value_out, extended, spectrum = rest[-5:]
    spectrum[...] = gains(med[...], analysis, pl.program_id(0))
    flag = (inner[1] if forward else inner[0]) > 0
    start = 0 if forward else near
    sign = -1 if forward else 1
    far_rows = kept(flag, halo[0:far, :].astype(jnp.float32)).astype(jnp.bfloat16)
    if forward:
        extended[0:length, :] = mix_grad[...]
        extended[length:, :] = far_rows
    else:
        extended[0:far, :] = far_rows
        extended[far:, :] = mix_grad[...]
    for at in range(0, columns, sub):
        cols = slice(at, at + sub)
        rim = kept(flag, halo[far:, cols].astype(jnp.float32))
        pieces = (gate_grad[:, cols], rim) if forward else (rim, gate_grad[:, cols])
        query_out[:, cols] = taps(pieces, weight[:, :, cols], 0, start, length, sign).astype(
            jnp.bfloat16
        )
    back = long_conv(extended, spectrum, analysis, synthesis, not forward)
    for at in range(0, columns, sub):
        cols = slice(at, at + sub)
        for member, feat, edge, out in (
            (1, value_feat, value_rim, key_out),
            (2, key_feat, key_rim, value_out),
        ):
            fix, beyond = edge[0:near, cols], edge[near:, cols]
            if forward:
                pieces = (fix, feat[near:, cols], beyond)
            else:
                pieces = (beyond, feat[: length - near, cols], fix)
            joined = jnp.concatenate([piece.astype(jnp.float32) for piece in pieces], axis=0)
            out[:, cols] = taps(
                (back[:, cols] * joined,), weight[:, :, cols], member, start, length, sign
            ).astype(jnp.bfloat16)


def final_kernel(terms, head, out):
    total = jnp.sum(terms[...], axis=0)
    out[...] = lax.dot_general(
        total[:4],
        head[...] * (1.0 / loss_scale),
        (((0,), (0,)), ((), ())),
        precision=lax.Precision.HIGHEST,
        preferred_element_type=jnp.float32,
    )


def per_device(query, key, value, stream, targets, short_filter, med_filter, out_weight, head):
    length = query.shape[1]
    channels = query.shape[2]
    half = channels // 2
    blocks = half // columns
    count = lax.axis_size("seq")
    owners = lax.axis_size("fsdp")
    own = half // owners
    rightward = [(i, (i + 1) % count) for i in range(count)]
    leftward = [((i + 1) % count, i) for i in range(count)]
    query, key, value, stream = query[0], key[0], value[0], stream[0]
    short_filter = in_hbm(short_filter.transpose(1, 0, 2))
    med_filter = in_hbm(med_filter)
    bf16, f32 = jnp.bfloat16, jnp.float32
    packed = reach + 5 * near
    shape = jax.ShapeDtypeStruct
    whole = pl.BlockSpec(memory_space=pltpu.VMEM)
    scalars = pl.BlockSpec(memory_space=pltpu.SMEM)
    untouched = pl.BlockSpec(memory_space=pl.ANY)
    query, key, value, stream = in_hbm(query), in_hbm(key), in_hbm(value), in_hbm(stream)
    limit = pltpu.CompilerParams(vmem_limit_bytes=vmem_limit)
    params = pltpu.CompilerParams(
        dimension_semantics=("arbitrary", "arbitrary"), vmem_limit_bytes=vmem_limit
    )

    def full(array):
        rank = len(array.shape)
        return pl.BlockSpec(array.shape, lambda *_: (0,) * rank)

    def by_channel(rows):
        return pl.BlockSpec((rows, columns), lambda b, s: (0, s * blocks + b))

    def edge_rows(first, last):
        return pl.BlockSpec(
            (near, columns), lambda b, s: (first + (last - first) * s, s * blocks + b)
        )

    def by_half(rows):
        return pl.BlockSpec((rows, columns), lambda b, s: (0, b))

    def by_owner(rows):
        return pl.BlockSpec((columns // lanes, rows, lanes), lambda b, s: (b, 0, 0))

    weight_spec = pl.BlockSpec(short_filter.shape[:2] + (columns,), lambda b, s: (0, 0, b))
    end = length // near - 1
    local_rows = shape((length, channels), bf16)
    hbm_rows = pltpu.HBM((length, channels), bf16)

    key_feat, value_feat, products, to_right, to_left = pl.pallas_call(
        functools.partial(local_kernel, length),
        grid=(blocks, 2),
        in_specs=[edge_rows(end, 0), by_channel(length), by_channel(length), weight_spec],
        out_specs=[by_channel(length)] * 3 + [by_half(packed)] * 2,
        out_shape=[hbm_rows] * 2 + [local_rows] + [shape((packed, half), bf16)] * 2,
        compiler_params=params,
        name="local_features",
    )(query, key, value, short_filter)

    from_left = lax.ppermute(to_right, "seq", rightward)
    from_right = lax.ppermute(to_left, "seq", leftward)

    shard, head_rows = pl.pallas_call(
        shard_kernel,
        in_specs=[whole] * 2,
        out_specs=[whole] * 2,
        out_shape=[shape((owners, parts, own), bf16), shape((parts, half), bf16)],
        compiler_params=limit,
        name="shard",
    )(out_weight, head)
    class_rows = lax.all_to_all(shard, "fsdp", 0, 0, tiled=True)
    if own != lanes:
        class_rows = class_rows.reshape(owners, parts, -1, lanes).transpose(0, 2, 1, 3)
        class_rows = class_rows.reshape(-1, parts, lanes)

    sums_shape = shape((2, length, parts), f32)
    first_gate, stream_sums = pl.pallas_call(
        functools.partial(gate_kernel, length),
        grid=(blocks, 2),
        in_specs=[by_channel(length)] * 2 + [weight_spec, by_half(parts)],
        out_specs=[by_channel(length), full(sums_shape)],
        out_shape=[local_rows, pltpu.HBM(sums_shape.shape, f32)],
        compiler_params=params,
        name="gate_and_stream_logits",
    )(query, stream, short_filter, head_rows)

    position = lax.axis_index("seq")
    inner = jnp.stack([position > 0, position < count - 1]).astype(jnp.int32)

    forward, inverse = dft_tables()
    analysis = jnp.asarray(np.concatenate(split_np(forward)))
    synth_c = jnp.asarray(np.concatenate(split_np(inverse[lead:])))
    synth_a = jnp.asarray(np.concatenate(split_np(inverse[:keep])))

    fold = np.zeros((2, parts, 128), np.float32)
    place = np.zeros((2, 2, 8, 2 * parts), np.float32)
    for lane in range(4):
        for part in range(3):
            fold[0, 4 * part + lane, lane] = 1.0
            fold[1, 4 * part + 3 - lane, lane] = 1.0
            for level in range(2):
                place[0, level, lane, level * parts + 4 * part + lane] = 1.0
                place[1, level, 3 - lane, level * parts + 4 * part + lane] = 1.0
    place = jnp.asarray(place.astype(ml_dtypes.bfloat16))

    grad_shape = shape((8, length), f32)
    gate, gated, mix, key_rim, value_rim, grad = pl.pallas_call(
        functools.partial(forward_kernel, length),
        grid=(blocks, 2),
        in_specs=[scalars, edge_rows(0, end)]
        + [edge_rows(0, 0), edge_rows(end, end)] * 2
        + [by_channel(length)] * 2
        + [by_half(packed)] * 2
        + [
            weight_spec, by_owner(parts), full(sums_shape), full(med_filter), full(targets),
            full(analysis), full(synth_c), full(synth_a), full(fold),
        ],
        out_specs=[by_channel(length)] * 3 + [by_channel(2 * near)] * 2 + [full(grad_shape)],
        out_shape=[local_rows] * 3 + [shape((2 * near, channels), bf16)] * 2 + [grad_shape],
        scratch_shapes=[
            pltpu.VMEM((span, columns), bf16),
            pltpu.VMEM((bins, columns), f32),
            pltpu.VMEM((2, length, parts), f32),
        ],
        compiler_params=params,
        name="mix_and_logits",
    )(
        inner, query, key, key, value, value, products, first_gate, from_left, from_right,
        short_filter, class_rows, stream_sums, med_filter, targets, analysis, synth_c, synth_a,
        jnp.asarray(fold),
    )

    partial, mix_grad, gate_grad, to_left, to_right = pl.pallas_call(
        functools.partial(middle_kernel, length),
        grid=(blocks, 2),
        in_specs=[by_channel(length)] * 3 + [by_owner(parts), full(grad), full(place)],
        out_specs=[by_owner(8)] + [by_channel(length)] * 2 + [by_half(far + near)] * 2,
        out_shape=[shape((half // lanes, 8, lanes), f32)]
        + [shape((length, channels), bf16)] * 2
        + [shape((far + near, half), bf16)] * 2,
        scratch_shapes=[
            pltpu.VMEM((2, 8, length), f32),
            pltpu.VMEM((2, length, 2 * parts), bf16),
        ],
        compiler_params=params,
        name="weight_partial_and_mix_grad",
    )(gate, gated, mix, class_rows, grad, place)

    grad_left = lax.ppermute(to_right, "seq", rightward)
    grad_right = lax.ppermute(to_left, "seq", leftward)
    if own != lanes:
        partial = partial.reshape(owners, -1, 8, lanes).transpose(0, 2, 1, 3)
        partial = partial.reshape(owners, 8, own)
    by_genome = lax.all_to_all(partial, "fsdp", 0, 0, tiled=True)

    def gradients(forward, mix_grad, halo, synthesis, earlier):
        base = 0 if forward else blocks

        def by_channel(rows):
            return pl.BlockSpec((rows, columns), lambda b: (0, base + b))

        in_specs = (
            [scalars]
            + [by_channel(length)] * 2
            + [pl.BlockSpec((far + near, columns), lambda b: (0, b))]
            + [by_channel(length)] * 2
            + [by_channel(2 * near)] * 2
            + [
                pl.BlockSpec(short_filter.shape[:2] + (columns,), lambda b: (0, 0, b)),
                full(med_filter), full(analysis), full(synthesis),
            ]
            + [untouched] * len(earlier)
        )
        taken = len(in_specs) - len(earlier)
        return pl.pallas_call(
            functools.partial(backward_kernel, length, forward),
            grid=(blocks,),
            in_specs=in_specs,
            out_specs=[by_channel(length)] * 3,
            out_shape=[local_rows] * 3,
            scratch_shapes=[pltpu.VMEM((span, columns), bf16), pltpu.VMEM((bins, columns), f32)],
            input_output_aliases={taken + at: at for at in range(len(earlier))},
            compiler_params=pltpu.CompilerParams(
                dimension_semantics=("arbitrary",), vmem_limit_bytes=vmem_limit
            ),
            name="gradients_forward" if forward else "gradients_reverse",
        )(
            inner, in_hbm(mix_grad), in_hbm(gate_grad), halo, in_hbm(key_feat),
            in_hbm(value_feat), key_rim, value_rim, short_filter, med_filter, analysis,
            synthesis, *earlier,
        )

    grads = gradients(True, mix_grad, grad_right, synth_a, ())
    by_genome, grads = lax.optimization_barrier((by_genome, tuple(grads)))
    over_genomes = jnp.sum(by_genome, axis=0)
    spread = jnp.broadcast_to(over_genomes, (count,) + over_genomes.shape)
    spread, mix_grad = lax.optimization_barrier((spread, mix_grad))
    terms = lax.all_to_all(spread, "seq", 0, 0, tiled=True)
    grads = gradients(False, mix_grad, grad_left, synth_c, grads)
    terms, grads = lax.optimization_barrier((terms, tuple(grads)))
    query_grad, key_grad, value_grad = grads
    out_grad = pl.pallas_call(
        final_kernel,
        in_specs=[whole] * 2,
        out_specs=whole,
        out_shape=shape((own, half), f32),
        compiler_params=limit,
        name="final",
    )(terms, head)
    return query_grad[None], key_grad[None], value_grad[None], out_grad


def solution(mesh):
    rows = P("fsdp", "seq", None)
    placed = (rows, rows, rows, rows, P("fsdp", "seq"), P(), P(), P("fsdp", None), P())
    return jax.shard_map(
        per_device,
        mesh=mesh,
        in_specs=placed,
        out_specs=(rows, rows, rows, P("fsdp", None)),
        check_vma=False,
    )
```

```python
import functools

import jax
import jax.numpy as jnp
import ml_dtypes
import numpy as np
from jax import lax
from jax.experimental import pallas as pl
from jax.experimental.pallas import tpu as pltpu
from jax.sharding import PartitionSpec as P

loss_scale = 64.0
far = 136
near = 8
reach = 128
span = 296
window = 216
step = 80
keep = 88
lead = window - keep
freqs = 112
bins = 2 * freqs
columns = 1024
per_group = 16
parts = 16
lanes = 128
sub = 128
vmem_limit = 34 * 1024 * 1024


def split_np(table):
    upper = table.astype(ml_dtypes.bfloat16)
    lower = (table - upper.astype(np.float64)).astype(ml_dtypes.bfloat16)
    return upper, lower


def dft_tables():
    omega = 2.0 * np.pi * (np.arange(freqs) + 0.5) / bins
    rows = np.arange(window)
    angles = omega[:, None] * rows
    forward = np.concatenate([np.cos(angles), -np.sin(angles)])
    return forward, forward.T / freqs


def split_bf16(value):
    upper = value.astype(jnp.bfloat16)
    return upper, (value - upper.astype(jnp.float32)).astype(jnp.bfloat16)


def dot(left, right):
    return jnp.dot(left, right, preferred_element_type=jnp.float32)


def dot_t(left, right):
    return lax.dot_general(
        left, right, (((1,), (1,)), ((), ())), preferred_element_type=jnp.float32
    )


def dot_ta(left, right):
    return lax.dot_general(
        left, right, (((0,), (0,)), ((), ())), preferred_element_type=jnp.float32
    )


def taps(pieces, weight, member, start, count, sign):
    rows = jnp.concatenate([piece.astype(jnp.float32) for piece in pieces], axis=0)
    total = rows.shape[0]
    tap = [weight[member, offset : offset + 1, :] for offset in range(7)]

    def moved(value, by):
        return pltpu.roll(value, (sign * by) % total, 0)

    one = moved(rows, 1)
    two = moved(rows, 2)
    tail = tap[4] * rows + tap[5] * one + tap[6] * two
    tail = tap[2] * rows + tap[3] * one + moved(tail, 2)
    tail = tap[0] * rows + tap[1] * one + moved(tail, 2)
    return tail[start : start + count]


def gains(med, analysis, block):
    groups = med.shape[1]
    channel = lax.broadcasted_iota(jnp.int32, (groups, columns), 1) + block * columns
    group = lax.broadcasted_iota(jnp.int32, (groups, columns), 0)
    expand = jnp.where(channel // per_group == group, 1.0, 0.0).astype(jnp.bfloat16)
    wide = dot(med, expand).astype(jnp.bfloat16)
    count = med.shape[0]
    both = dot(analysis[:, :count], wide)
    return both[:bins] + both[bins:]


def in_hbm(array):
    return pltpu.with_memory_space_constraint(array, pltpu.HBM)


def thirds(value):
    first, rest = split_bf16(value)
    second = (value - first.astype(jnp.float32)).astype(jnp.bfloat16)
    third = (value - first.astype(jnp.float32) - second.astype(jnp.float32)).astype(jnp.bfloat16)
    pieces = [piece.astype(jnp.float32) for piece in (first, second, third)]
    blank = jnp.zeros((parts - 12, value.shape[1]), jnp.float32)
    return jnp.concatenate(pieces + [blank], axis=0).astype(jnp.bfloat16)


def shard_kernel(out_weight, head, shard_out, head_out):
    coded = thirds(head[...])
    head_out[...] = coded
    found = dot_t(coded, out_weight[...])
    shard = thirds(found[0:4] + found[4:8] + found[8:12])
    for device in range(shard_out.shape[0]):
        shard_out[device] = shard


def local_kernel(
    length, q_edge, k, v, weight, key_out, value_out, products_out, to_right, to_left
):
    side = pl.program_id(1)

    def one(forward):
        sign = 1 if forward else -1
        for at in range(0, columns, sub):
            cols = slice(at, at + sub)
            taken = weight[:, :, cols]
            key_feat = taps((k[:, cols],), taken, 1, 0, length, sign)
            value_feat = taps((v[:, cols],), taken, 2, 0, length, sign)
            key_out[:, cols] = key_feat.astype(jnp.bfloat16)
            value_out[:, cols] = value_feat.astype(jnp.bfloat16)
            products_out[:, cols] = (key_feat * value_feat).astype(jnp.bfloat16)
        main, other = (to_right, to_left) if forward else (to_left, to_right)
        main_at = length - near if forward else 0
        other_at = 0 if forward else length - near
        first = length - reach if forward else 0
        main[0:reach, :] = products_out[first : first + reach, :]
        main[reach : reach + near, :] = q_edge[...]
        main[reach + near : reach + 2 * near, :] = k[main_at : main_at + near, :]
        main[reach + 2 * near : reach + 3 * near, :] = v[main_at : main_at + near, :]
        other[reach + 3 * near : reach + 4 * near, :] = k[other_at : other_at + near, :]
        other[reach + 4 * near : reach + 5 * near, :] = v[other_at : other_at + near, :]

    pl.when(side == 0)(functools.partial(one, True))
    pl.when(side == 1)(functools.partial(one, False))


def gate_kernel(length, q, s, weight, head_rows, gate_out, sums_out):
    block = pl.program_id(0)
    side = pl.program_id(1)

    def one(forward):
        for at in range(0, columns, sub):
            cols = slice(at, at + sub)
            gate = taps((q[:, cols],), weight[:, :, cols], 0, 0, length, 1 if forward else -1)
            gate_out[:, cols] = gate.astype(jnp.bfloat16)
        side_at = 0 if forward else 1
        term = dot_t(s[...], head_rows[...])

        @pl.when(block == 0)
        def _():
            sums_out[side_at] = term

        @pl.when(block > 0)
        def _():
            sums_out[side_at] += term

    pl.when(side == 0)(functools.partial(one, True))
    pl.when(side == 1)(functools.partial(one, False))


def class_block(class_rows):
    return jnp.concatenate([class_rows[piece] for piece in range(class_rows.shape[0])], axis=1)


def long_conv(rows_ref, spectrum, analysis, synthesis, causal):
    gain_re = spectrum[0:freqs, :]
    gain_im = spectrum[freqs:bins, :]
    if not causal:
        gain_im = -gain_im
    pieces = []
    for index in range(2):
        both = dot(analysis[...], rows_ref[index * step : index * step + window, :])
        re = both[:freqs] + both[bins : bins + freqs]
        im = both[freqs:bins] + both[bins + freqs :]
        mixed = jnp.concatenate([re * gain_re - im * gain_im, re * gain_im + im * gain_re], axis=0)
        both = dot(synthesis[...], mixed.astype(jnp.bfloat16))
        piece = both[:keep] + both[keep:]
        pieces.append(piece[:step] if index == 0 else piece)
    return jnp.concatenate(pieces, axis=0)


def kept(flag, piece):
    return jnp.where(flag, piece, jnp.zeros_like(piece))


def forward_kernel(
    length, inner, q_edge, k_low, k_high, v_low, v_high, local, first_gate, left, right, weight,
    class_rows, stream_sums, med, target, analysis, synth_c, synth_a, fold,
    gate_out, gated_out, mix_out, key_rim, value_rim, grad_out,
    products, spectrum, sums,
):
    block = pl.program_id(0)
    side = pl.program_id(1)

    @pl.when((block == 0) & (side == 0))
    def _():
        sums[...] = stream_sums[...]

    @pl.when(side == 0)
    def _():
        spectrum[...] = gains(med[...], analysis, block)

    def one(forward):
        main, other = (left, right) if forward else (right, left)
        left_flag, right_flag = inner[0] > 0, inner[1] > 0
        main_flag, other_flag = (left_flag, right_flag) if forward else (right_flag, left_flag)
        sign = 1 if forward else -1
        wide = jnp.float32

        def edges(low, high, member):
            at = reach + member * near
            beside_main = kept(main_flag, main[at : at + near, :].astype(wide))
            at = reach + (2 + member) * near
            beside_other = kept(other_flag, other[at : at + near, :].astype(wide))
            before, after = (
                (beside_main, beside_other) if forward else (beside_other, beside_main)
            )
            found = taps(
                (before, low[...], high[...], after), weight, member, 0, 4 * near, sign
            )
            if forward:
                return found[near : 2 * near], found[3 * near :]
            return found[2 * near : 3 * near], found[:near]

        key_fix, key_beyond = edges(k_low, k_high, 1)
        value_fix, value_beyond = edges(v_low, v_high, 2)
        key_rim[0:near, :] = key_fix.astype(jnp.bfloat16)
        key_rim[near:, :] = key_beyond.astype(jnp.bfloat16)
        value_rim[0:near, :] = value_fix.astype(jnp.bfloat16)
        value_rim[near:, :] = value_beyond.astype(jnp.bfloat16)
        halo = kept(main_flag, main[0:reach, :].astype(wide)).astype(jnp.bfloat16)
        fixed = (key_fix * value_fix).astype(jnp.bfloat16)
        beyond = (key_beyond * value_beyond).astype(jnp.bfloat16)
        q_near = kept(main_flag, main[reach : reach + near, :].astype(wide))
        if forward:
            products[0:reach, :] = halo
            products[reach : reach + near, :] = fixed
            products[reach + near : reach + length, :] = local[near:, :]
            products[reach + length :, :] = beyond
            gate = taps((q_near, q_edge[...]), weight, 0, near, near, sign)
            gate_out[0:near, :] = gate.astype(jnp.bfloat16)
            gate_out[near:, :] = first_gate[near:, :]
        else:
            products[0:near, :] = beyond
            products[near:length, :] = local[: length - near, :]
            products[length : length + near, :] = fixed
            products[length + near :, :] = halo
            gate = taps((q_edge[...], q_near), weight, 0, 0, near, sign)
            gate_out[0 : length - near, :] = first_gate[: length - near, :]
            gate_out[length - near :, :] = gate.astype(jnp.bfloat16)
        mix = long_conv(products, spectrum, analysis, synth_c if forward else synth_a, forward)
        mix = mix[:length] if forward else mix[near:]
        mix_out[...] = mix.astype(jnp.bfloat16)
        gated = (gate_out[...].astype(jnp.float32) * mix).astype(jnp.bfloat16)
        gated_out[...] = gated
        sums[0 if forward else 1] += dot_t(gated, class_block(class_rows))

    pl.when(side == 0)(functools.partial(one, True))
    pl.when(side == 1)(functools.partial(one, False))

    @pl.when((block == pl.num_programs(0) - 1) & (side == 1))
    def _():
        exact = lax.Precision.HIGHEST
        logits = jnp.dot(
            sums[0], fold[0], precision=exact, preferred_element_type=jnp.float32
        ) + jnp.dot(sums[1], fold[1], precision=exact, preferred_element_type=jnp.float32)
        logits = jnp.transpose(logits)[:8]
        row = lax.broadcasted_iota(jnp.int32, logits.shape, 0)
        valid = row < 4
        top = jnp.max(jnp.where(valid, logits, -jnp.inf), axis=0, keepdims=True)
        exponent = jnp.where(valid, jnp.exp(logits - top), 0.0)
        softmax_out = exponent / jnp.sum(exponent, axis=0, keepdims=True)
        one_hot = jnp.where(row == target[...], 1.0, 0.0)
        grad_out[...] = loss_scale * (softmax_out - one_hot)


def middle_kernel(
    length, gate, gated, mix, class_rows, grad, place,
    partial_out, mix_grad_out, gate_grad_out, to_left, to_right,
    turned, coded,
):
    block = pl.program_id(0)
    side = pl.program_id(1)

    @pl.when((block == 0) & (side == 0))
    def _():
        high, low = split_bf16(grad[...])
        for side_at in range(2):
            coded[side_at] = (
                dot_ta(high, place[side_at, 0]) + dot_ta(low, place[side_at, 1])
            ).astype(jnp.bfloat16)
        turned[0] = grad[...]
        for lane in range(4):
            turned[1, lane : lane + 1, :] = grad[3 - lane : 4 - lane, :]
        turned[1, 4:8, :] = jnp.zeros((4, length), jnp.float32)

    def one(forward):
        high, low = split_bf16(turned[0 if forward else 1])
        term = dot(high, gated[...]) + dot(low, gated[...])
        for piece in range(columns // lanes):
            cut = term[:, piece * lanes : piece * lanes + lanes]
            if forward:
                partial_out[piece] = cut
            else:
                partial_out[piece] += cut
        classes = class_block(class_rows)
        grads = dot(coded[0 if forward else 1], jnp.concatenate([classes, classes], axis=0))
        mix_grad = (grads * gate[...].astype(jnp.float32)).astype(jnp.bfloat16)
        gate_grad = (grads * mix[...].astype(jnp.float32)).astype(jnp.bfloat16)
        mix_grad_out[...] = mix_grad
        gate_grad_out[...] = gate_grad
        if forward:
            to_left[0:far, :] = mix_grad[:far]
            to_left[far:, :] = gate_grad[:near]
        else:
            to_right[0:far, :] = mix_grad[length - far :]
            to_right[far:, :] = gate_grad[length - near :]

    pl.when(side == 0)(functools.partial(one, True))
    pl.when(side == 1)(functools.partial(one, False))


def backward_kernel(
    length, forward, inner, mix_grad, gate_grad, halo, key_feat, value_feat, key_rim, value_rim,
    weight, med, analysis, synthesis, *rest,
):
    query_out, key_out, value_out, extended, spectrum = rest[-5:]
    spectrum[...] = gains(med[...], analysis, pl.program_id(0))
    flag = (inner[1] if forward else inner[0]) > 0
    start = 0 if forward else near
    sign = -1 if forward else 1
    far_rows = kept(flag, halo[0:far, :].astype(jnp.float32)).astype(jnp.bfloat16)
    if forward:
        extended[0:length, :] = mix_grad[...]
        extended[length:, :] = far_rows
    else:
        extended[0:far, :] = far_rows
        extended[far:, :] = mix_grad[...]
    for at in range(0, columns, sub):
        cols = slice(at, at + sub)
        rim = kept(flag, halo[far:, cols].astype(jnp.float32))
        pieces = (gate_grad[:, cols], rim) if forward else (rim, gate_grad[:, cols])
        query_out[:, cols] = taps(pieces, weight[:, :, cols], 0, start, length, sign).astype(
            jnp.bfloat16
        )
    back = long_conv(extended, spectrum, analysis, synthesis, not forward)
    for at in range(0, columns, sub):
        cols = slice(at, at + sub)
        for member, feat, edge, out in (
            (1, value_feat, value_rim, key_out),
            (2, key_feat, key_rim, value_out),
        ):
            fix, beyond = edge[0:near, cols], edge[near:, cols]
            if forward:
                pieces = (fix, feat[near:, cols], beyond)
            else:
                pieces = (beyond, feat[: length - near, cols], fix)
            joined = jnp.concatenate([piece.astype(jnp.float32) for piece in pieces], axis=0)
            out[:, cols] = taps(
                (back[:, cols] * joined,), weight[:, :, cols], member, start, length, sign
            ).astype(jnp.bfloat16)


def final_kernel(terms, head, out):
    total = jnp.sum(terms[...], axis=0)
    out[...] = lax.dot_general(
        total[:4],
        head[...] * (1.0 / loss_scale),
        (((0,), (0,)), ((), ())),
        precision=lax.Precision.HIGHEST,
        preferred_element_type=jnp.float32,
    )


def per_device(query, key, value, stream, targets, short_filter, med_filter, out_weight, head):
    length = query.shape[1]
    channels = query.shape[2]
    half = channels // 2
    blocks = half // columns
    count = lax.axis_size("seq")
    owners = lax.axis_size("fsdp")
    own = half // owners
    rightward = [(i, (i + 1) % count) for i in range(count)]
    leftward = [((i + 1) % count, i) for i in range(count)]
    query, key, value, stream = query[0], key[0], value[0], stream[0]
    short_filter = in_hbm(short_filter.transpose(1, 0, 2))
    med_filter = in_hbm(med_filter)
    bf16, f32 = jnp.bfloat16, jnp.float32
    packed = reach + 5 * near
    shape = jax.ShapeDtypeStruct
    whole = pl.BlockSpec(memory_space=pltpu.VMEM)
    scalars = pl.BlockSpec(memory_space=pltpu.SMEM)
    untouched = pl.BlockSpec(memory_space=pl.ANY)
    query, key, value, stream = in_hbm(query), in_hbm(key), in_hbm(value), in_hbm(stream)
    limit = pltpu.CompilerParams(vmem_limit_bytes=vmem_limit)
    params = pltpu.CompilerParams(
        dimension_semantics=("arbitrary", "arbitrary"), vmem_limit_bytes=vmem_limit
    )

    def full(array):
        rank = len(array.shape)
        return pl.BlockSpec(array.shape, lambda *_: (0,) * rank)

    def by_channel(rows):
        return pl.BlockSpec((rows, columns), lambda b, s: (0, s * blocks + b))

    def edge_rows(first, last):
        return pl.BlockSpec(
            (near, columns), lambda b, s: (first + (last - first) * s, s * blocks + b)
        )

    def by_half(rows):
        return pl.BlockSpec((rows, columns), lambda b, s: (0, b))

    def by_owner(rows):
        return pl.BlockSpec((columns // lanes, rows, lanes), lambda b, s: (b, 0, 0))

    weight_spec = pl.BlockSpec(short_filter.shape[:2] + (columns,), lambda b, s: (0, 0, b))
    end = length // near - 1
    local_rows = shape((length, channels), bf16)
    hbm_rows = pltpu.HBM((length, channels), bf16)

    key_feat, value_feat, products, to_right, to_left = pl.pallas_call(
        functools.partial(local_kernel, length),
        grid=(blocks, 2),
        in_specs=[edge_rows(end, 0), by_channel(length), by_channel(length), weight_spec],
        out_specs=[by_channel(length)] * 3 + [by_half(packed)] * 2,
        out_shape=[hbm_rows] * 2 + [local_rows] + [shape((packed, half), bf16)] * 2,
        compiler_params=params,
        name="local_features",
    )(query, key, value, short_filter)

    from_left = lax.ppermute(to_right, "seq", rightward)
    from_right = lax.ppermute(to_left, "seq", leftward)

    shard, head_rows = pl.pallas_call(
        shard_kernel,
        in_specs=[whole] * 2,
        out_specs=[whole] * 2,
        out_shape=[shape((owners, parts, own), bf16), shape((parts, half), bf16)],
        compiler_params=limit,
        name="shard",
    )(out_weight, head)
    class_rows = lax.all_to_all(shard, "fsdp", 0, 0, tiled=True)
    if own != lanes:
        class_rows = class_rows.reshape(owners, parts, -1, lanes).transpose(0, 2, 1, 3)
        class_rows = class_rows.reshape(-1, parts, lanes)

    sums_shape = shape((2, length, parts), f32)
    first_gate, stream_sums = pl.pallas_call(
        functools.partial(gate_kernel, length),
        grid=(blocks, 2),
        in_specs=[by_channel(length)] * 2 + [weight_spec, by_half(parts)],
        out_specs=[by_channel(length), full(sums_shape)],
        out_shape=[local_rows, pltpu.HBM(sums_shape.shape, f32)],
        compiler_params=params,
        name="gate_and_stream_logits",
    )(query, stream, short_filter, head_rows)

    position = lax.axis_index("seq")
    inner = jnp.stack([position > 0, position < count - 1]).astype(jnp.int32)

    forward, inverse = dft_tables()
    analysis = in_hbm(jnp.asarray(np.concatenate(split_np(forward))))
    synth_c = in_hbm(jnp.asarray(np.concatenate(split_np(inverse[lead:]))))
    synth_a = in_hbm(jnp.asarray(np.concatenate(split_np(inverse[:keep]))))

    fold = np.zeros((2, parts, 128), np.float32)
    place = np.zeros((2, 2, 8, 2 * parts), np.float32)
    for lane in range(4):
        for part in range(3):
            fold[0, 4 * part + lane, lane] = 1.0
            fold[1, 4 * part + 3 - lane, lane] = 1.0
            for level in range(2):
                place[0, level, lane, level * parts + 4 * part + lane] = 1.0
                place[1, level, 3 - lane, level * parts + 4 * part + lane] = 1.0
    place = in_hbm(jnp.asarray(place.astype(ml_dtypes.bfloat16)))

    grad_shape = shape((8, length), f32)
    gate, gated, mix, key_rim, value_rim, grad = pl.pallas_call(
        functools.partial(forward_kernel, length),
        grid=(blocks, 2),
        in_specs=[scalars, edge_rows(0, end)]
        + [edge_rows(0, 0), edge_rows(end, end)] * 2
        + [by_channel(length)] * 2
        + [by_half(packed)] * 2
        + [
            weight_spec, by_owner(parts), full(sums_shape), full(med_filter), full(targets),
            full(analysis), full(synth_c), full(synth_a), full(fold),
        ],
        out_specs=[by_channel(length)] * 3 + [by_channel(2 * near)] * 2 + [full(grad_shape)],
        out_shape=[local_rows] * 3 + [pltpu.HBM((2 * near, channels), bf16)] * 2 + [grad_shape],
        scratch_shapes=[
            pltpu.VMEM((span, columns), bf16),
            pltpu.VMEM((bins, columns), f32),
            pltpu.VMEM((2, length, parts), f32),
        ],
        compiler_params=params,
        name="mix_and_logits",
    )(
        inner, query, key, key, value, value, products, first_gate, from_left, from_right,
        short_filter, class_rows, in_hbm(stream_sums), med_filter, in_hbm(targets), analysis, synth_c, synth_a,
        in_hbm(jnp.asarray(fold)),
    )

    partial, mix_grad, gate_grad, to_left, to_right = pl.pallas_call(
        functools.partial(middle_kernel, length),
        grid=(blocks, 2),
        in_specs=[by_channel(length)] * 3 + [by_owner(parts), full(grad), full(place)],
        out_specs=[by_owner(8)] + [by_channel(length)] * 2 + [by_half(far + near)] * 2,
        out_shape=[shape((half // lanes, 8, lanes), f32)]
        + [shape((length, channels), bf16)] * 2
        + [shape((far + near, half), bf16)] * 2,
        scratch_shapes=[
            pltpu.VMEM((2, 8, length), f32),
            pltpu.VMEM((2, length, 2 * parts), bf16),
        ],
        compiler_params=params,
        name="weight_partial_and_mix_grad",
    )(gate, gated, mix, class_rows, grad, place)

    grad_left = lax.ppermute(to_right, "seq", rightward)
    grad_right = lax.ppermute(to_left, "seq", leftward)
    if own != lanes:
        partial = partial.reshape(owners, -1, 8, lanes).transpose(0, 2, 1, 3)
        partial = partial.reshape(owners, 8, own)
    by_genome = lax.all_to_all(partial, "fsdp", 0, 0, tiled=True)

    def gradients(forward, mix_grad, halo, synthesis, earlier):
        base = 0 if forward else blocks

        def by_channel(rows):
            return pl.BlockSpec((rows, columns), lambda b: (0, base + b))

        in_specs = (
            [scalars]
            + [by_channel(length)] * 2
            + [pl.BlockSpec((far + near, columns), lambda b: (0, b))]
            + [by_channel(length)] * 2
            + [by_channel(2 * near)] * 2
            + [
                pl.BlockSpec(short_filter.shape[:2] + (columns,), lambda b: (0, 0, b)),
                full(med_filter), full(analysis), full(synthesis),
            ]
            + [untouched] * len(earlier)
        )
        taken = len(in_specs) - len(earlier)
        return pl.pallas_call(
            functools.partial(backward_kernel, length, forward),
            grid=(blocks,),
            in_specs=in_specs,
            out_specs=[by_channel(length)] * 3,
            out_shape=[local_rows] * 3,
            scratch_shapes=[pltpu.VMEM((span, columns), bf16), pltpu.VMEM((bins, columns), f32)],
            input_output_aliases={taken + at: at for at in range(len(earlier))},
            compiler_params=pltpu.CompilerParams(
                dimension_semantics=("arbitrary",), vmem_limit_bytes=vmem_limit
            ),
            name="gradients_forward" if forward else "gradients_reverse",
        )(
            inner, mix_grad, gate_grad, halo, in_hbm(key_feat),
            in_hbm(value_feat), in_hbm(key_rim), in_hbm(value_rim), short_filter, med_filter, analysis,
            synthesis, *earlier,
        )

    grads = gradients(True, mix_grad, grad_right, synth_a, ())
    by_genome, grads = lax.optimization_barrier((by_genome, tuple(grads)))
    over_genomes = jnp.sum(by_genome, axis=0)
    spread = jnp.broadcast_to(over_genomes, (count,) + over_genomes.shape)
    spread, mix_grad = lax.optimization_barrier((spread, mix_grad))
    terms = lax.all_to_all(spread, "seq", 0, 0, tiled=True)
    grads = gradients(False, mix_grad, grad_left, synth_c, grads)
    terms, grads = lax.optimization_barrier((terms, tuple(grads)))
    query_grad, key_grad, value_grad = grads
    out_grad = pl.pallas_call(
        final_kernel,
        in_specs=[whole] * 2,
        out_specs=whole,
        out_shape=shape((own, half), f32),
        compiler_params=limit,
        name="final",
    )(terms, head)
    return query_grad[None], key_grad[None], value_grad[None], out_grad


def solution(mesh):
    rows = P("fsdp", "seq", None)
    placed = (rows, rows, rows, rows, P("fsdp", "seq"), P(), P(), P("fsdp", None), P())
    return jax.shard_map(
        per_device,
        mesh=mesh,
        in_specs=placed,
        out_specs=(rows, rows, rows, P("fsdp", None)),
        check_vma=False,
    )
```

```python
import functools

import jax
import jax.numpy as jnp
import ml_dtypes
import numpy as np
from jax import lax
from jax.experimental import pallas as pl
from jax.experimental.pallas import tpu as pltpu
from jax.sharding import PartitionSpec as P

loss_scale = 64.0
far = 136
near = 8
reach = 128
span = 296
window = 216
step = 80
keep = 88
lead = window - keep
freqs = 112
bins = 2 * freqs
columns = 1024
per_group = 16
parts = 16
lanes = 128
sub = 128
vmem_limit = 34 * 1024 * 1024


def split_np(table):
    upper = table.astype(ml_dtypes.bfloat16)
    lower = (table - upper.astype(np.float64)).astype(ml_dtypes.bfloat16)
    return upper, lower


def dft_tables():
    omega = 2.0 * np.pi * (np.arange(freqs) + 0.5) / bins
    rows = np.arange(window)
    angles = omega[:, None] * rows
    forward = np.concatenate([np.cos(angles), -np.sin(angles)])
    return forward, forward.T / freqs


def split_bf16(value):
    upper = value.astype(jnp.bfloat16)
    return upper, (value - upper.astype(jnp.float32)).astype(jnp.bfloat16)


def dot(left, right):
    return jnp.dot(left, right, preferred_element_type=jnp.float32)


def dot_t(left, right):
    return lax.dot_general(
        left, right, (((1,), (1,)), ((), ())), preferred_element_type=jnp.float32
    )


def dot_ta(left, right):
    return lax.dot_general(
        left, right, (((0,), (0,)), ((), ())), preferred_element_type=jnp.float32
    )


def taps(pieces, weight, member, start, count, sign):
    rows = jnp.concatenate([piece.astype(jnp.float32) for piece in pieces], axis=0)
    total = rows.shape[0]
    tap = [weight[member, offset : offset + 1, :] for offset in range(7)]

    def moved(value, by):
        return pltpu.roll(value, (sign * by) % total, 0)

    one = moved(rows, 1)
    two = moved(rows, 2)
    tail = tap[4] * rows + tap[5] * one + tap[6] * two
    tail = tap[2] * rows + tap[3] * one + moved(tail, 2)
    tail = tap[0] * rows + tap[1] * one + moved(tail, 2)
    return tail[start : start + count]


def gains(med, analysis, block):
    groups = med.shape[1]
    channel = lax.broadcasted_iota(jnp.int32, (groups, columns), 1) + block * columns
    group = lax.broadcasted_iota(jnp.int32, (groups, columns), 0)
    expand = jnp.where(channel // per_group == group, 1.0, 0.0).astype(jnp.bfloat16)
    wide = dot(med, expand).astype(jnp.bfloat16)
    count = med.shape[0]
    both = dot(analysis[:, :count], wide)
    return both[:bins] + both[bins:]


def in_hbm(array):
    return pltpu.with_memory_space_constraint(array, pltpu.HBM)


def thirds(value):
    first, rest = split_bf16(value)
    second = (value - first.astype(jnp.float32)).astype(jnp.bfloat16)
    third = (value - first.astype(jnp.float32) - second.astype(jnp.float32)).astype(jnp.bfloat16)
    pieces = [piece.astype(jnp.float32) for piece in (first, second, third)]
    blank = jnp.zeros((parts - 12, value.shape[1]), jnp.float32)
    return jnp.concatenate(pieces + [blank], axis=0).astype(jnp.bfloat16)


def shard_kernel(out_weight, head, shard_out, head_out):
    coded = thirds(head[...])
    head_out[...] = coded
    found = dot_t(coded, out_weight[...])
    shard = thirds(found[0:4] + found[4:8] + found[8:12])
    for device in range(shard_out.shape[0]):
        shard_out[device] = shard


def local_kernel(
    length, q_edge, k, v, weight, key_out, value_out, products_out, to_right, to_left
):
    side = pl.program_id(1)

    def one(forward):
        sign = 1 if forward else -1
        for at in range(0, columns, sub):
            cols = slice(at, at + sub)
            taken = weight[:, :, cols]
            key_feat = taps((k[:, cols],), taken, 1, 0, length, sign)
            value_feat = taps((v[:, cols],), taken, 2, 0, length, sign)
            key_out[:, cols] = key_feat.astype(jnp.bfloat16)
            value_out[:, cols] = value_feat.astype(jnp.bfloat16)
            products_out[:, cols] = (key_feat * value_feat).astype(jnp.bfloat16)
        main, other = (to_right, to_left) if forward else (to_left, to_right)
        main_at = length - near if forward else 0
        other_at = 0 if forward else length - near
        first = length - reach if forward else 0
        main[0:reach, :] = products_out[first : first + reach, :]
        main[reach : reach + near, :] = q_edge[...]
        main[reach + near : reach + 2 * near, :] = k[main_at : main_at + near, :]
        main[reach + 2 * near : reach + 3 * near, :] = v[main_at : main_at + near, :]
        other[reach + 3 * near : reach + 4 * near, :] = k[other_at : other_at + near, :]
        other[reach + 4 * near : reach + 5 * near, :] = v[other_at : other_at + near, :]

    pl.when(side == 0)(functools.partial(one, True))
    pl.when(side == 1)(functools.partial(one, False))


def gate_kernel(length, q, s, weight, head_rows, gate_out, sums_out):
    block = pl.program_id(0)
    side = pl.program_id(1)

    def one(forward):
        for at in range(0, columns, sub):
            cols = slice(at, at + sub)
            gate = taps((q[:, cols],), weight[:, :, cols], 0, 0, length, 1 if forward else -1)
            gate_out[:, cols] = gate.astype(jnp.bfloat16)
        side_at = 0 if forward else 1
        term = dot_t(s[...], head_rows[...])

        @pl.when(block == 0)
        def _():
            sums_out[side_at] = term

        @pl.when(block > 0)
        def _():
            sums_out[side_at] += term

    pl.when(side == 0)(functools.partial(one, True))
    pl.when(side == 1)(functools.partial(one, False))


def class_block(class_rows):
    return jnp.concatenate([class_rows[piece] for piece in range(class_rows.shape[0])], axis=1)


def long_conv(rows_ref, spectrum, analysis, synthesis, causal):
    gain_re = spectrum[0:freqs, :]
    gain_im = spectrum[freqs:bins, :]
    if not causal:
        gain_im = -gain_im
    pieces = []
    for index in range(2):
        both = dot(analysis[...], rows_ref[index * step : index * step + window, :])
        re = both[:freqs] + both[bins : bins + freqs]
        im = both[freqs:bins] + both[bins + freqs :]
        mixed = jnp.concatenate([re * gain_re - im * gain_im, re * gain_im + im * gain_re], axis=0)
        both = dot(synthesis[...], mixed.astype(jnp.bfloat16))
        piece = both[:keep] + both[keep:]
        pieces.append(piece[:step] if index == 0 else piece)
    return jnp.concatenate(pieces, axis=0)


def kept(flag, piece):
    return jnp.where(flag, piece, jnp.zeros_like(piece))


def forward_kernel(
    length, inner, q_edge, k_low, k_high, v_low, v_high, local, first_gate, left, right, weight,
    class_rows, stream_sums, med, target, analysis, synth_c, synth_a, fold,
    gate_out, gated_out, mix_out, key_rim, value_rim, grad_out,
    products, spectrum, sums,
):
    block = pl.program_id(0)
    side = pl.program_id(1)

    @pl.when((block == 0) & (side == 0))
    def _():
        sums[...] = stream_sums[...]

    @pl.when(side == 0)
    def _():
        spectrum[...] = gains(med[...], analysis, block)

    def one(forward):
        main, other = (left, right) if forward else (right, left)
        left_flag, right_flag = inner[0] > 0, inner[1] > 0
        main_flag, other_flag = (left_flag, right_flag) if forward else (right_flag, left_flag)
        sign = 1 if forward else -1
        wide = jnp.float32

        def edges(low, high, member):
            at = reach + member * near
            beside_main = kept(main_flag, main[at : at + near, :].astype(wide))
            at = reach + (2 + member) * near
            beside_other = kept(other_flag, other[at : at + near, :].astype(wide))
            before, after = (
                (beside_main, beside_other) if forward else (beside_other, beside_main)
            )
            found = taps(
                (before, low[...], high[...], after), weight, member, 0, 4 * near, sign
            )
            if forward:
                return found[near : 2 * near], found[3 * near :]
            return found[2 * near : 3 * near], found[:near]

        key_fix, key_beyond = edges(k_low, k_high, 1)
        value_fix, value_beyond = edges(v_low, v_high, 2)
        key_rim[0:near, :] = key_fix.astype(jnp.bfloat16)
        key_rim[near:, :] = key_beyond.astype(jnp.bfloat16)
        value_rim[0:near, :] = value_fix.astype(jnp.bfloat16)
        value_rim[near:, :] = value_beyond.astype(jnp.bfloat16)
        halo = kept(main_flag, main[0:reach, :].astype(wide)).astype(jnp.bfloat16)
        fixed = (key_fix * value_fix).astype(jnp.bfloat16)
        beyond = (key_beyond * value_beyond).astype(jnp.bfloat16)
        q_near = kept(main_flag, main[reach : reach + near, :].astype(wide))
        if forward:
            products[0:reach, :] = halo
            products[reach : reach + near, :] = fixed
            products[reach + near : reach + length, :] = local[near:, :]
            products[reach + length :, :] = beyond
            gate = taps((q_near, q_edge[...]), weight, 0, near, near, sign)
            gate_out[0:near, :] = gate.astype(jnp.bfloat16)
            gate_out[near:, :] = first_gate[near:, :]
        else:
            products[0:near, :] = beyond
            products[near:length, :] = local[: length - near, :]
            products[length : length + near, :] = fixed
            products[length + near :, :] = halo
            gate = taps((q_edge[...], q_near), weight, 0, 0, near, sign)
            gate_out[0 : length - near, :] = first_gate[: length - near, :]
            gate_out[length - near :, :] = gate.astype(jnp.bfloat16)
        mix = long_conv(products, spectrum, analysis, synth_c if forward else synth_a, forward)
        mix = mix[:length] if forward else mix[near:]
        mix_out[...] = mix.astype(jnp.bfloat16)
        gated = (gate_out[...].astype(jnp.float32) * mix).astype(jnp.bfloat16)
        gated_out[...] = gated
        sums[0 if forward else 1] += dot_t(gated, class_block(class_rows))

    pl.when(side == 0)(functools.partial(one, True))
    pl.when(side == 1)(functools.partial(one, False))

    @pl.when((block == pl.num_programs(0) - 1) & (side == 1))
    def _():
        exact = lax.Precision.HIGHEST
        logits = jnp.dot(
            sums[0], fold[0], precision=exact, preferred_element_type=jnp.float32
        ) + jnp.dot(sums[1], fold[1], precision=exact, preferred_element_type=jnp.float32)
        logits = jnp.transpose(logits)[:8]
        row = lax.broadcasted_iota(jnp.int32, logits.shape, 0)
        valid = row < 4
        top = jnp.max(jnp.where(valid, logits, -jnp.inf), axis=0, keepdims=True)
        exponent = jnp.where(valid, jnp.exp(logits - top), 0.0)
        softmax_out = exponent / jnp.sum(exponent, axis=0, keepdims=True)
        one_hot = jnp.where(row == target[...], 1.0, 0.0)
        grad_out[...] = loss_scale * (softmax_out - one_hot)


def middle_kernel(
    length, gate, gated, mix, class_rows, grad, place,
    partial_out, mix_grad_out, gate_grad_out, to_left, to_right,
    turned, coded,
):
    block = pl.program_id(0)
    side = pl.program_id(1)

    @pl.when((block == 0) & (side == 0))
    def _():
        high, low = split_bf16(grad[...])
        for side_at in range(2):
            coded[side_at] = (
                dot_ta(high, place[side_at, 0]) + dot_ta(low, place[side_at, 1])
            ).astype(jnp.bfloat16)
        turned[0] = grad[...]
        for lane in range(4):
            turned[1, lane : lane + 1, :] = grad[3 - lane : 4 - lane, :]
        turned[1, 4:8, :] = jnp.zeros((4, length), jnp.float32)

    def one(forward):
        high, low = split_bf16(turned[0 if forward else 1])
        term = dot(high, gated[...]) + dot(low, gated[...])
        for piece in range(columns // lanes):
            cut = term[:, piece * lanes : piece * lanes + lanes]
            if forward:
                partial_out[piece] = cut
            else:
                partial_out[piece] += cut
        classes = class_block(class_rows)
        grads = dot(coded[0 if forward else 1], jnp.concatenate([classes, classes], axis=0))
        mix_grad = (grads * gate[...].astype(jnp.float32)).astype(jnp.bfloat16)
        gate_grad = (grads * mix[...].astype(jnp.float32)).astype(jnp.bfloat16)
        mix_grad_out[...] = mix_grad
        gate_grad_out[...] = gate_grad
        if forward:
            to_left[0:far, :] = mix_grad[:far]
            to_left[far:, :] = gate_grad[:near]
        else:
            to_right[0:far, :] = mix_grad[length - far :]
            to_right[far:, :] = gate_grad[length - near :]

    pl.when(side == 0)(functools.partial(one, True))
    pl.when(side == 1)(functools.partial(one, False))


def backward_kernel(
    length, forward, inner, mix_grad, gate_grad, halo, key_feat, value_feat, key_rim, value_rim,
    weight, med, analysis, synthesis, *rest,
):
    query_out, key_out, value_out, extended, spectrum = rest[-5:]
    spectrum[...] = gains(med[...], analysis, pl.program_id(0))
    flag = (inner[1] if forward else inner[0]) > 0
    start = 0 if forward else near
    sign = -1 if forward else 1
    far_rows = kept(flag, halo[0:far, :].astype(jnp.float32)).astype(jnp.bfloat16)
    if forward:
        extended[0:length, :] = mix_grad[...]
        extended[length:, :] = far_rows
    else:
        extended[0:far, :] = far_rows
        extended[far:, :] = mix_grad[...]
    for at in range(0, columns, sub):
        cols = slice(at, at + sub)
        rim = kept(flag, halo[far:, cols].astype(jnp.float32))
        pieces = (gate_grad[:, cols], rim) if forward else (rim, gate_grad[:, cols])
        query_out[:, cols] = taps(pieces, weight[:, :, cols], 0, start, length, sign).astype(
            jnp.bfloat16
        )
    back = long_conv(extended, spectrum, analysis, synthesis, not forward)
    for at in range(0, columns, sub):
        cols = slice(at, at + sub)
        for member, feat, edge, out in (
            (1, value_feat, value_rim, key_out),
            (2, key_feat, key_rim, value_out),
        ):
            fix, beyond = edge[0:near, cols], edge[near:, cols]
            if forward:
                pieces = (fix, feat[near:, cols], beyond)
            else:
                pieces = (beyond, feat[: length - near, cols], fix)
            joined = jnp.concatenate([piece.astype(jnp.float32) for piece in pieces], axis=0)
            out[:, cols] = taps(
                (back[:, cols] * joined,), weight[:, :, cols], member, start, length, sign
            ).astype(jnp.bfloat16)


def final_kernel(terms, head_rows, out):
    total = jnp.sum(terms[...], axis=0)[:4] * (1.0 / loss_scale)
    coded = thirds(total).astype(jnp.float32)
    heads = head_rows[...].astype(jnp.float32)
    pairs = ((0, 0), (0, 1), (1, 0), (1, 1), (0, 2), (2, 0))
    left = jnp.concatenate([coded[4 * a : 4 * a + 4] for a, _ in pairs], axis=0)
    right = jnp.concatenate([heads[4 * b : 4 * b + 4] for _, b in pairs], axis=0)
    out[...] = dot_ta(left.astype(jnp.bfloat16), right.astype(jnp.bfloat16))


def per_device(query, key, value, stream, targets, short_filter, med_filter, out_weight, head):
    length = query.shape[1]
    channels = query.shape[2]
    half = channels // 2
    blocks = half // columns
    count = lax.axis_size("seq")
    owners = lax.axis_size("fsdp")
    own = half // owners
    rightward = [(i, (i + 1) % count) for i in range(count)]
    leftward = [((i + 1) % count, i) for i in range(count)]
    query, key, value, stream = query[0], key[0], value[0], stream[0]
    short_filter = in_hbm(short_filter.transpose(1, 0, 2))
    med_filter = in_hbm(med_filter)
    bf16, f32 = jnp.bfloat16, jnp.float32
    packed = reach + 5 * near
    shape = jax.ShapeDtypeStruct
    whole = pl.BlockSpec(memory_space=pltpu.VMEM)
    scalars = pl.BlockSpec(memory_space=pltpu.SMEM)
    untouched = pl.BlockSpec(memory_space=pl.ANY)
    query, key, value, stream = in_hbm(query), in_hbm(key), in_hbm(value), in_hbm(stream)
    limit = pltpu.CompilerParams(vmem_limit_bytes=vmem_limit)
    params = pltpu.CompilerParams(
        dimension_semantics=("arbitrary", "arbitrary"), vmem_limit_bytes=vmem_limit
    )

    def full(array):
        rank = len(array.shape)
        return pl.BlockSpec(array.shape, lambda *_: (0,) * rank)

    def by_channel(rows):
        return pl.BlockSpec((rows, columns), lambda b, s: (0, s * blocks + b))

    def edge_rows(first, last):
        return pl.BlockSpec(
            (near, columns), lambda b, s: (first + (last - first) * s, s * blocks + b)
        )

    def by_half(rows):
        return pl.BlockSpec((rows, columns), lambda b, s: (0, b))

    def by_owner(rows):
        return pl.BlockSpec((columns // lanes, rows, lanes), lambda b, s: (b, 0, 0))

    weight_spec = pl.BlockSpec(short_filter.shape[:2] + (columns,), lambda b, s: (0, 0, b))
    end = length // near - 1
    local_rows = shape((length, channels), bf16)
    hbm_rows = pltpu.HBM((length, channels), bf16)

    key_feat, value_feat, products, to_right, to_left = pl.pallas_call(
        functools.partial(local_kernel, length),
        grid=(blocks, 2),
        in_specs=[edge_rows(end, 0), by_channel(length), by_channel(length), weight_spec],
        out_specs=[by_channel(length)] * 3 + [by_half(packed)] * 2,
        out_shape=[hbm_rows] * 2 + [local_rows] + [shape((packed, half), bf16)] * 2,
        compiler_params=params,
        name="local_features",
    )(query, key, value, short_filter)

    from_left = lax.ppermute(to_right, "seq", rightward)
    from_right = lax.ppermute(to_left, "seq", leftward)

    shard, head_rows = pl.pallas_call(
        shard_kernel,
        in_specs=[whole] * 2,
        out_specs=[whole] * 2,
        out_shape=[shape((owners, parts, own), bf16), shape((parts, half), bf16)],
        compiler_params=limit,
        name="shard",
    )(out_weight, head)
    class_rows = lax.all_to_all(shard, "fsdp", 0, 0, tiled=True)
    if own != lanes:
        class_rows = class_rows.reshape(owners, parts, -1, lanes).transpose(0, 2, 1, 3)
        class_rows = class_rows.reshape(-1, parts, lanes)

    sums_shape = shape((2, length, parts), f32)
    first_gate, stream_sums = pl.pallas_call(
        functools.partial(gate_kernel, length),
        grid=(blocks, 2),
        in_specs=[by_channel(length)] * 2 + [weight_spec, by_half(parts)],
        out_specs=[by_channel(length), full(sums_shape)],
        out_shape=[local_rows, pltpu.HBM(sums_shape.shape, f32)],
        compiler_params=params,
        name="gate_and_stream_logits",
    )(query, stream, short_filter, head_rows)

    position = lax.axis_index("seq")
    inner = jnp.stack([position > 0, position < count - 1]).astype(jnp.int32)

    forward, inverse = dft_tables()
    analysis = in_hbm(jnp.asarray(np.concatenate(split_np(forward))))
    synth_c = in_hbm(jnp.asarray(np.concatenate(split_np(inverse[lead:]))))
    synth_a = in_hbm(jnp.asarray(np.concatenate(split_np(inverse[:keep]))))

    fold = np.zeros((2, parts, 128), np.float32)
    place = np.zeros((2, 2, 8, 2 * parts), np.float32)
    for lane in range(4):
        for part in range(3):
            fold[0, 4 * part + lane, lane] = 1.0
            fold[1, 4 * part + 3 - lane, lane] = 1.0
            for level in range(2):
                place[0, level, lane, level * parts + 4 * part + lane] = 1.0
                place[1, level, 3 - lane, level * parts + 4 * part + lane] = 1.0
    place = in_hbm(jnp.asarray(place.astype(ml_dtypes.bfloat16)))

    grad_shape = shape((8, length), f32)
    gate, gated, mix, key_rim, value_rim, grad = pl.pallas_call(
        functools.partial(forward_kernel, length),
        grid=(blocks, 2),
        in_specs=[scalars, edge_rows(0, end)]
        + [edge_rows(0, 0), edge_rows(end, end)] * 2
        + [by_channel(length)] * 2
        + [by_half(packed)] * 2
        + [
            weight_spec, by_owner(parts), full(sums_shape), full(med_filter), full(targets),
            full(analysis), full(synth_c), full(synth_a), full(fold),
        ],
        out_specs=[by_channel(length)] * 3 + [by_channel(2 * near)] * 2 + [full(grad_shape)],
        out_shape=[local_rows] * 3 + [pltpu.HBM((2 * near, channels), bf16)] * 2 + [grad_shape],
        scratch_shapes=[
            pltpu.VMEM((span, columns), bf16),
            pltpu.VMEM((bins, columns), f32),
            pltpu.VMEM((2, length, parts), f32),
        ],
        compiler_params=params,
        name="mix_and_logits",
    )(
        inner, query, key, key, value, value, products, first_gate, from_left, from_right,
        short_filter, class_rows, in_hbm(stream_sums), med_filter, in_hbm(targets), analysis, synth_c, synth_a,
        in_hbm(jnp.asarray(fold)),
    )

    partial, mix_grad, gate_grad, to_left, to_right = pl.pallas_call(
        functools.partial(middle_kernel, length),
        grid=(blocks, 2),
        in_specs=[by_channel(length)] * 3 + [by_owner(parts), full(grad), full(place)],
        out_specs=[by_owner(8)] + [by_channel(length)] * 2 + [by_half(far + near)] * 2,
        out_shape=[shape((half // lanes, 8, lanes), f32)]
        + [shape((length, channels), bf16)] * 2
        + [shape((far + near, half), bf16)] * 2,
        scratch_shapes=[
            pltpu.VMEM((2, 8, length), f32),
            pltpu.VMEM((2, length, 2 * parts), bf16),
        ],
        compiler_params=params,
        name="weight_partial_and_mix_grad",
    )(gate, gated, mix, class_rows, grad, place)

    grad_left = lax.ppermute(to_right, "seq", rightward)
    grad_right = lax.ppermute(to_left, "seq", leftward)
    if own != lanes:
        partial = partial.reshape(owners, -1, 8, lanes).transpose(0, 2, 1, 3)
        partial = partial.reshape(owners, 8, own)
    by_genome = lax.all_to_all(partial, "fsdp", 0, 0, tiled=True)

    def gradients(forward, mix_grad, halo, synthesis, earlier):
        base = 0 if forward else blocks

        def by_channel(rows):
            return pl.BlockSpec((rows, columns), lambda b: (0, base + b))

        in_specs = (
            [scalars]
            + [by_channel(length)] * 2
            + [pl.BlockSpec((far + near, columns), lambda b: (0, b))]
            + [by_channel(length)] * 2
            + [by_channel(2 * near)] * 2
            + [
                pl.BlockSpec(short_filter.shape[:2] + (columns,), lambda b: (0, 0, b)),
                full(med_filter), full(analysis), full(synthesis),
            ]
            + [untouched] * len(earlier)
        )
        taken = len(in_specs) - len(earlier)
        return pl.pallas_call(
            functools.partial(backward_kernel, length, forward),
            grid=(blocks,),
            in_specs=in_specs,
            out_specs=[by_channel(length)] * 3,
            out_shape=[local_rows] * 3,
            scratch_shapes=[pltpu.VMEM((span, columns), bf16), pltpu.VMEM((bins, columns), f32)],
            input_output_aliases={taken + at: at for at in range(len(earlier))},
            compiler_params=pltpu.CompilerParams(
                dimension_semantics=("arbitrary",), vmem_limit_bytes=vmem_limit
            ),
            name="gradients_forward" if forward else "gradients_reverse",
        )(
            inner, mix_grad, gate_grad, halo, in_hbm(key_feat),
            in_hbm(value_feat), in_hbm(key_rim), in_hbm(value_rim), short_filter, med_filter, analysis,
            synthesis, *earlier,
        )

    grads = gradients(True, mix_grad, grad_right, synth_a, ())
    by_genome, grads = lax.optimization_barrier((by_genome, tuple(grads)))
    over_genomes = jnp.sum(by_genome, axis=0)
    spread = jnp.broadcast_to(over_genomes, (count,) + over_genomes.shape)
    spread, mix_grad = lax.optimization_barrier((spread, mix_grad))
    terms = lax.all_to_all(spread, "seq", 0, 0, tiled=True)
    grads = gradients(False, mix_grad, grad_left, synth_c, grads)
    terms, grads = lax.optimization_barrier((terms, tuple(grads)))
    query_grad, key_grad, value_grad = grads
    out_grad = pl.pallas_call(
        final_kernel,
        grid=(blocks,),
        in_specs=[full(terms), pl.BlockSpec((parts, columns), lambda b: (0, b))],
        out_specs=pl.BlockSpec((own, columns), lambda b: (0, b)),
        out_shape=shape((own, half), f32),
        compiler_params=pltpu.CompilerParams(
            dimension_semantics=("arbitrary",), vmem_limit_bytes=vmem_limit
        ),
        name="final",
    )(terms, head_rows)
    return query_grad[None], key_grad[None], value_grad[None], out_grad


def solution(mesh):
    rows = P("fsdp", "seq", None)
    placed = (rows, rows, rows, rows, P("fsdp", "seq"), P(), P(), P("fsdp", None), P())
    return jax.shard_map(
        per_device,
        mesh=mesh,
        in_specs=placed,
        out_specs=(rows, rows, rows, P("fsdp", None)),
        check_vma=False,
    )
```
